128 devices in a mesh: cell: 2 (over core), panel: 2 (over x_lo), sc: 32 (over z, y, x_hi).
Axes of the slice: x: 4 (x_hi: 2, x_lo: 2; x = x_hi * 2 + x_lo), y: 4, z: 4, core: 2. Of those that a mesh axis runs over, the one named last changes fastest.
Arguments:
- channel: bfloat16 [4, 1024, 2, 1024, 128], P('cell', 'sc', None, 'panel'), may hold values from -0.1875 to 0.1875
- received: bfloat16 [4, 1024, 2, 14, 1024], P('cell', 'sc', None, None, 'panel'), may hold values from -6 to 6
- noise_power: float32 [4], P('cell'), may hold values from 0.05 to 0.5
- user_count: int32 [4, 64], P('cell', 'sc'), may hold values from 32 to 128
- serving_cell: int32 [4, 128, 1], P('cell'), may hold values from 0 to 3; in each aligned block of 256 rows (0 to 255, 256 to 511, ..., all dimensions but the last counted through in order) at most 128 rows name the same one
Outputs:
- routed_symbols: bfloat16 [4, 256, 2, 14, 1024], P('cell', 'sc')
The draws below stay inside these ranges and needn't reach their ends.
Inputs may be any that keep to these rules, and one draw needn't show every extreme that they name: `serving_cell`: at most 128 user slots of one block of 2 consecutive cells name the same serving cell, and in every draw some serving cell is named exactly 128 times by one block.
All inputs are finite; a program needn't handle non-finite values.
Results may differ from the reference program's by a relative error of at most 0.0057.
Values may be sent and summed in bfloat16 or wider, within the bound.
A program may use at most 128 MiB of HBM per device.

```python
import math
import jax
import jax.numpy as jnp
import numpy as np
from jax import lax

CELLS_PER_PART = 2
ANTENNA_COUNT = 1024
USER_SLOTS = 128
SYMBOL_COUNT = 14
GRP = 16
ITERS = 2
CELL_COUNT = 4
SUBCARRIER_COUNT = 1024
GROUPS = 64
CAP = 128
SLOTS = 256
N_CELL = 2


def plant(result, key, smallest, top_value):
    longest = result.shape.index(max(result.shape))
    spots = []
    for shift in (0, 1):
        where = [jax.random.randint(jax.random.fold_in(key, axis), (), 0, length) for axis, length in enumerate(result.shape)]
        where[longest] = (where[longest] + shift) % result.shape[longest]
        spots.append(tuple(where))
    return result.at[spots[0]].set(smallest).at[spots[1]].set(top_value)


def levels(key, extent, cuts, least, largest):
    level, own = 1.0, jax.random.fold_in(key, 6)
    for axis_at, parts in cuts:
        heights = jnp.exp(jax.random.uniform(jax.random.fold_in(own, axis_at), (parts,), jnp.float32, least / len(cuts), largest / len(cuts)))
        level = level * jnp.repeat(heights, extent[axis_at] // parts).reshape([-1 if axis == axis_at else 1 for axis in range(len(extent))])
    return level


def shared_out(own_key, own, number, rows, count, top, bound, slope):
    order = jax.random.permutation(own_key, count)
    crowded, common = load_shares(count, rows * top, bound, slope, True), load_shares(count, rows * top, bound, slope, False)
    places = jnp.arange(count)

    def named(sizes, turn):
        used = int((sizes > 0).sum())
        fixed = max(1, used // 4)
        moved = fixed + (places - fixed + turn * (used - fixed)) % max(1, count - fixed)
        return jnp.zeros((count,), jnp.int32).at[order[jnp.where(places < fixed, places, moved)]].set(jnp.asarray(sizes, jnp.int32))

    sizes = jnp.where(number % 4 == 0, named(crowded, number // 4), named(common, number - number // 4 - 1))
    mixed = jax.random.permutation(jax.random.fold_in(own, 3), count)
    donor, sink = mixed[0:count // 2 * 2:2], mixed[1:count // 2 * 2:2]
    room = jnp.minimum(sizes[donor] - 1, bound - sizes[sink]) // 2
    room = jnp.where((donor == order[0]) | (sink == order[0]) | (sizes[sink] == 0), 0, jnp.maximum(room, 0))
    moved = jax.random.randint(jax.random.fold_in(own, 4), (count // 2,), 0, 1 << 20) % (room + 1)
    sizes = sizes.at[donor].add(-moved).at[sink].add(moved)
    labels = jnp.searchsorted(jnp.cumsum(sizes), jnp.arange(rows * top), side="right").astype(jnp.int32)
    grid = labels.reshape(top, rows).T
    grid = grid[jax.random.permutation(jax.random.fold_in(own, 1), rows)]
    turn = jax.random.randint(jax.random.fold_in(own, 2), (rows, 1), 0, top)
    return jnp.take_along_axis(grid, (jnp.arange(top)[None, :] + turn) % top, axis=1)


def load_shares(amount, total, bound, lean, full):
    portions = [(1 << 20) // math.isqrt(standing ** lean) + 1 for standing in range(1, amount + 1)]
    largest = bound if full else min(bound, max(-(-total // amount), total * portions[0] // sum(portions)))
    least = 1 if total - largest >= amount - 1 else 0
    given, rest = [largest] + [least] * (amount - 1), total - largest - least * (amount - 1)
    while rest > 0:
        movable = [i for i in range(1, amount) if given[i] < largest] or [i for i in range(1, amount) if given[i] < bound]
        pool, budget = sum([portions[i] for i in movable]), rest
        for i in movable:
            addition = min(bound - given[i], max(1, budget * portions[i] // pool), rest)
            given[i] = given[i] + addition
            rest = rest - addition
    return np.array(given)


def gaussian(own_key, shape, scale, reach, pieces=(), held_as=jnp.bfloat16):
    entries = scale * jax.random.normal(own_key, shape, jnp.float32)
    if pieces:
        entries = entries * levels(own_key, shape, pieces, -0.22, 0.18)
    return jnp.clip(entries, -reach, reach).astype(held_as)


def setup_inputs(seed: int = 0) -> dict:
    seeds = jax.random.split(jax.random.key(seed), 6)
    channel = gaussian(seeds[0], (CELL_COUNT, SUBCARRIER_COUNT, 2, ANTENNA_COUNT, USER_SLOTS), ANTENNA_COUNT ** -0.5, 0.1875, ((0, 2), (1, 32), (3, 2)))
    received = gaussian(seeds[1], (CELL_COUNT, SUBCARRIER_COUNT, 2, SYMBOL_COUNT, ANTENNA_COUNT), 1.0, 6.0, ((0, 2), (1, 32), (4, 2)))
    noise_power = jnp.clip(jnp.exp(math.log(0.5) - 2.3025851 * jax.random.uniform(seeds[2], (CELL_COUNT,), jnp.float32) ** levels(seeds[2], (CELL_COUNT,), ((0, 2),), -0.2, 0.2)), 0.05, 0.5)
    user_count = plant(jax.random.randint(seeds[3], (CELL_COUNT, GROUPS), USER_SLOTS // 4, USER_SLOTS + 1), jax.random.fold_in(seeds[3], 1), USER_SLOTS // 4, USER_SLOTS).astype(jnp.int32)
    serving_cell_keys = jax.random.split(jax.random.fold_in(seeds[4], 1), CELL_COUNT * USER_SLOTS // (CELLS_PER_PART * USER_SLOTS))
    serving_cell_turns = jax.random.permutation(jax.random.fold_in(seeds[4], 3), CELL_COUNT * USER_SLOTS // (CELLS_PER_PART * USER_SLOTS))
    serving_cell = jax.vmap(lambda own, number: shared_out(jax.random.fold_in(seeds[4], 2), own, number, CELLS_PER_PART * USER_SLOTS, CELL_COUNT, 1, CAP, 2))(serving_cell_keys, serving_cell_turns).reshape((CELL_COUNT, USER_SLOTS, 1))
    return {"channel": channel, "received": received, "noise_power": noise_power, "user_count": user_count, "serving_cell": serving_cell}


def adjoint_apply(matrix, vector):
    products = jnp.einsum('faku,fbsk->fabsu', matrix, vector, precision=lax.Precision.HIGHEST)
    return jnp.stack((products[:, 0, 0] + products[:, 1, 1], products[:, 0, 1] - products[:, 1, 0]), axis=1)


def apply_channel(matrix, vector):
    products = jnp.einsum('faku,fbsu->fabsk', matrix, vector, precision=lax.Precision.HIGHEST)
    return jnp.stack((products[:, 0, 0] - products[:, 1, 1], products[:, 0, 1] + products[:, 1, 0]), axis=1)


def round_half(values):
    return lax.optimization_barrier(values.astype(jnp.bfloat16)).astype(jnp.float32)


def user_sum(left, right):
    return jnp.sum(left * right, axis=(1, 3))


def widen(values):
    return values[:, None, :, None]


def detect_cell(inputs):
    channel, received, noise, counts = inputs
    matrix = channel.astype(jnp.float32)
    padded = jnp.pad(matrix, ((1, 1), (0, 0), (0, 0), (0, 0)))
    index = jnp.arange(SUBCARRIER_COUNT)
    weight = jnp.where((index == 0) | (index == SUBCARRIER_COUNT - 1), 0.75, 1.0).astype(jnp.float32)
    smooth = (0.25 * padded[:-2] + 0.5 * padded[1:-1] + 0.25 * padded[2:]) / weight[:, None, None, None]
    active = (jnp.arange(USER_SLOTS)[None, :] < counts[:, None]).astype(jnp.float32)
    smoothed = round_half(smooth * active[:, None, None, :])
    matched = adjoint_apply(smoothed, received.astype(jnp.float32))
    estimate = jnp.zeros_like(matched)
    residual = matched
    direction = matched
    norm_now = user_sum(residual, residual)
    for iteration in range(ITERS):
        column_image = round_half(apply_channel(smoothed, round_half(direction)))
        image = adjoint_apply(smoothed, column_image) + noise * direction
        alpha = norm_now / user_sum(direction, image)
        estimate = estimate + widen(alpha) * direction
        residual = residual - widen(alpha) * image
        norm_next = user_sum(residual, residual)
        direction = residual + widen(norm_next / norm_now) * direction
        norm_now = norm_next
    return estimate


def reference(channel, received, noise_power, user_count, serving_cell):
    counts = jnp.repeat(user_count, GRP, axis=1)
    estimate = lax.map(detect_cell, (channel, received, noise_power, counts))
    detected = estimate.astype(jnp.bfloat16)
    keys = serving_cell[:, :, 0].astype(jnp.int32)
    block_list = keys.reshape(N_CELL, CELLS_PER_PART * USER_SLOTS)
    position = jnp.arange(CELLS_PER_PART * USER_SLOTS)
    earlier = (block_list[:, :, None] == block_list[:, None, :]) & (position[None, None, :] < position[None, :, None])
    rank = jnp.sum(earlier.astype(jnp.int32), axis=2).reshape(-1).astype(jnp.int32)
    source = (jnp.arange(CELL_COUNT * USER_SLOTS) // (CELLS_PER_PART * USER_SLOTS)).astype(jnp.int32)
    target = (keys.reshape(-1) * SLOTS + source * CAP + rank).astype(jnp.int32)
    symbols = detected.transpose(0, 4, 2, 3, 1).reshape(CELL_COUNT * USER_SLOTS, 2, SYMBOL_COUNT, SUBCARRIER_COUNT)
    routed = jnp.zeros((CELL_COUNT * SLOTS, 2, SYMBOL_COUNT, SUBCARRIER_COUNT), jnp.bfloat16).at[target].set(symbols)
    return routed.reshape(CELL_COUNT, SLOTS, 2, SYMBOL_COUNT, SUBCARRIER_COUNT)
```

```python
import functools

import jax
import jax.numpy as jnp
from jax import lax
from jax.experimental import pallas as pl
from jax.experimental.pallas import tpu as pltpu
from jax.sharding import PartitionSpec as P

GRP = 16
MESH = pl.DeviceIdType.MESH
F32, BF16 = jnp.float32, jnp.bfloat16

BAND, ANT, USERS, SYM = 32, 512, 128, 14
INNER = BAND - 2
SIZE = 10
PER_CELL = INNER // SIZE
GROUPS = 2 * PER_CELL
UNITS = 2 * BAND


def adjoint(rows, block):
    out = jnp.dot(rows, block, preferred_element_type=F32)
    real = out[:16, :128] + out[16:, 128:]
    imag = out[16:, :128] - out[:16, 128:]
    return real, imag


def forward(real, imag, block):
    left = jnp.concatenate(
        [jnp.concatenate([real, -imag], axis=1), jnp.concatenate([imag, real], axis=1)], axis=0
    )
    return lax.dot_general(left, block, (((1,), (1,)), ((), ())), preferred_element_type=F32)


def row_sum(values):
    return jnp.sum(values, axis=1, keepdims=True)


def detect_kernel(
    channel, received, noise, counts, keys, out,
    raw, smooth, rx, halo, msend, mrecv, isend, irecv, qsend, qrecv, norm1, dirsq, first, second, det,
    raw_sem, rx_sem, halo_ssem, halo_rsem, m_ssem, m_rsem, i_ssem, i_rsem, q_ssem, q_rsem,
):
    c_id, p_id, s_id = lax.axis_index("cell"), lax.axis_index("panel"), lax.axis_index("sc")
    n_sc = lax.axis_size("sc")
    partner = (c_id, 1 - p_id, s_id)
    upper = (c_id, p_id, lax.rem(s_id + 1, n_sc))
    lower = (c_id, p_id, lax.rem(s_id + n_sc - 1, n_sc))

    def raw_copy(c, k):
        rows = pl.ds(k * SIZE + 2, SIZE)
        return pltpu.make_async_copy(channel.at[c, rows], raw.at[c, rows], raw_sem.at[c, k])

    def head_copy(c):
        rows = pl.ds(0, 2)
        return pltpu.make_async_copy(channel.at[c, rows], raw.at[c, rows], raw_sem.at[c, PER_CELL])

    def rx_copy(c):
        return pltpu.make_async_copy(
            received.at[c], rx.at[c], rx_sem.at[c]
        )

    for c in range(2):
        head_copy(c).start()
        rx_copy(c).start()
        for k in range(PER_CELL):
            raw_copy(c, k).start()

    barrier = pltpu.get_barrier_semaphore()
    for device in (partner, upper, lower):
        pl.semaphore_signal(barrier, inc=1, device_id=device, device_id_type=MESH)
    pl.semaphore_wait(barrier, 3)

    halo_copies = []
    for c in range(2):
        for side, (edge, device) in enumerate(((BAND - 1, upper), (0, lower))):
            halo_copies.append(
                pltpu.make_async_remote_copy(
                    src_ref=channel.at[c, edge],
                    dst_ref=halo.at[c, side],
                    send_sem=halo_ssem.at[c, side],
                    recv_sem=halo_rsem.at[c, side],
                    device_id=device,
                    device_id_type=MESH,
                )
            )
    for copy in halo_copies:
        copy.start()

    def exchange(source, target, ssem, rsem, start, size, slot):
        return pltpu.make_async_remote_copy(
            src_ref=source.at[pl.ds(start, size)],
            dst_ref=target.at[pl.ds(start, size)],
            send_sem=ssem.at[slot],
            recv_sem=rsem.at[slot],
            device_id=partner,
            device_id_type=MESH,
        )

    def group_copy(pair, g):
        source, target, ssem, rsem = pair
        return exchange(source, target, ssem, rsem, g * SIZE, SIZE, g)

    def edge_copy(pair):
        source, target, ssem, rsem = pair
        return exchange(source, target, ssem, rsem, GROUPS * SIZE, 4, GROUPS)

    m_pair = (msend, mrecv, m_ssem, m_rsem)
    i_pair = (isend, irecv, i_ssem, i_rsem)
    lane = lax.broadcasted_iota(jnp.int32, (16, 128), 1)

    def mask_of(c, f):
        return lane < counts[c, f // GRP]

    STRIP = 64

    def smooth_block(n, low, mid, high, low_gain, high_gain):
        for part in range(2):
            for row in range(0, ANT, STRIP):
                rows = pl.ds(row, STRIP)
                a = low[part, rows, :].astype(F32)
                b = mid[part, rows, :].astype(F32)
                d = high[part, rows, :].astype(F32)
                if low_gain is not None:
                    a = a * low_gain
                if high_gain is not None:
                    d = d * high_gain
                smooth[n, rows, pl.ds(128 * part, 128)] = (a + d + (b + b)).astype(BF16)

    def matched_terms(n, c, f, gain):
        real, imag = adjoint(rx[c, f].reshape(32, ANT), smooth[n])
        msend[n, 0] = (real * gain).astype(BF16)
        msend[n, 1] = (imag * gain).astype(BF16)

    def matched(n):
        real = msend[n, 0].astype(F32) + mrecv[n, 0].astype(F32)
        imag = msend[n, 1].astype(F32) + mrecv[n, 1].astype(F32)
        return real, imag

    def image_terms(n, c, f, gain):
        keep = mask_of(c, f)
        real, imag = matched(n)
        real, imag = jnp.where(keep, real, 0.0), jnp.where(keep, imag, 0.0)
        column = forward(real.astype(BF16), imag.astype(BF16), smooth[n])
        column = (column * gain).astype(BF16)
        real, imag = adjoint(column, smooth[n])
        isend[n, 0] = (real * gain).astype(BF16)
        isend[n, 1] = (imag * gain).astype(BF16)

    def second_terms(n, c, f, gain):
        keep = mask_of(c, f)
        power = noise[c]
        br, bi = matched(n)
        br, bi = jnp.where(keep, br, 0.0), jnp.where(keep, bi, 0.0)
        ir = isend[n, 0].astype(F32) + irecv[n, 0].astype(F32)
        ii = isend[n, 1].astype(F32) + irecv[n, 1].astype(F32)
        ir = jnp.where(keep, ir, 0.0) + power * br
        ii = jnp.where(keep, ii, 0.0) + power * bi
        norm0 = row_sum(br * br + bi * bi)
        alpha = norm0 / row_sum(br * ir + bi * ii)
        er, ei = alpha * br, alpha * bi
        rr, ri = br - alpha * ir, bi - alpha * ii
        norm = row_sum(rr * rr + ri * ri)
        beta = norm / norm0
        dr, di = rr + beta * br, ri + beta * bi
        first[n, 0], first[n, 1] = er, ei
        second[n, 0], second[n, 1] = dr, di
        column = forward(dr.astype(BF16), di.astype(BF16), smooth[n]) * gain
        square = column * column
        square = square[:16] + square[16:]
        square = (square[:, :128] + square[:, 128:256]) + (square[:, 256:384] + square[:, 384:])
        here = lane == n
        qsend[...] = jnp.where(here, row_sum(square), qsend[...])
        norm1[...] = jnp.where(here, norm, norm1[...])
        dirsq[...] = jnp.where(here, power * row_sum(dr * dr + di * di), dirsq[...])

    low_end, high_end = s_id == 0, s_id == n_sc - 1
    edge_gain = (
        jnp.where(low_end, 1.0 / 3.0, 0.25).astype(F32),
        jnp.where(high_end, 1.0 / 3.0, 0.25).astype(F32),
    )
    halo_gain = (jnp.where(low_end, 0.0, 1.0).astype(F32), jnp.where(high_end, 0.0, 1.0).astype(F32))

    def each_inner(g, run, unroll):
        c = g // PER_CELL
        base = lax.rem(g, PER_CELL) * SIZE + 1

        def step(i, _):
            for k in range(unroll):
                run(g * SIZE + i * unroll + k, c, base + i * unroll + k, 0.25)
            return 0

        lax.fori_loop(0, SIZE // unroll, step, 0)

    def each_edge(run):
        def step(c, _):
            for side in range(2):
                run(GROUPS * SIZE + 2 * c + side, c, side * (BAND - 1), edge_gain[side])
            return 0

        lax.fori_loop(0, 2, step, 0)

    for c in range(2):
        head_copy(c).wait()
        rx_copy(c).wait()

    def first_unit(n, c, f, gain):
        smooth_block(n, raw.at[c, f - 1], raw.at[c, f], raw.at[c, f + 1], None, None)
        matched_terms(n, c, f, gain)

    def first_phase(g, _):
        raw_copy(g // PER_CELL, lax.rem(g, PER_CELL)).wait()
        each_inner(g, first_unit, 1)
        group_copy(m_pair, g).start()
        return 0

    lax.fori_loop(0, GROUPS, first_phase, 0)

    def image_phase(g, _):
        group_copy(m_pair, g).wait()
        each_inner(g, image_terms, 5)
        group_copy(i_pair, g).start()
        return 0

    def second_phase(g, _):
        group_copy(i_pair, g).wait()
        each_inner(g, second_terms, 5)
        return 0

    for copy in halo_copies:
        copy.wait()

    def edge_first(c, _):
        for side in range(2):
            n = GROUPS * SIZE + 2 * c + side
            f = side * (BAND - 1)
            if side == 0:
                smooth_block(n, halo.at[c, 0], raw.at[c, 0], raw.at[c, 1], halo_gain[0], None)
            else:
                smooth_block(n, raw.at[c, f - 1], raw.at[c, f], halo.at[c, 1], None, halo_gain[1])
            matched_terms(n, c, f, edge_gain[side])
        return 0

    lax.fori_loop(0, 2, edge_first, 0)
    edge_copy(m_pair).start()

    lax.fori_loop(0, GROUPS, image_phase, 0)
    edge_copy(m_pair).wait()
    each_edge(image_terms)
    edge_copy(i_pair).start()

    qsend[...] = jnp.zeros_like(qsend)
    norm1[...] = jnp.ones_like(norm1)
    dirsq[...] = jnp.ones_like(dirsq)
    lax.fori_loop(0, GROUPS, second_phase, 0)
    edge_copy(i_pair).wait()
    each_edge(second_terms)

    q_copy = pltpu.make_async_remote_copy(
        src_ref=qsend, dst_ref=qrecv, send_sem=q_ssem, recv_sem=q_rsem,
        device_id=partner, device_id_type=MESH,
    )
    q_copy.start()

    key = keys[...]
    users2 = 2 * USERS
    rows_i = lax.broadcasted_iota(jnp.int32, (users2, users2), 0)
    cols_i = lax.broadcasted_iota(jnp.int32, (users2, users2), 1)
    key_f = key.astype(F32)
    key_row = jnp.sum(jnp.where(rows_i == cols_i, key_f, 0.0), axis=0, keepdims=True)
    earlier = (key_f == key_row) & (rows_i < cols_i)
    rank_row = jnp.sum(jnp.where(earlier, 1.0, 0.0), axis=0, keepdims=True).astype(jnp.int32)
    key_row = key_row.astype(jnp.int32)
    place = (key_row // 2) * 256 + (rank_row // 8) * 16 + lax.rem(key_row, 2) * 8 + lax.rem(rank_row, 8)

    q_copy.wait()
    alpha1 = norm1[...] / (qsend[...] + qrecv[...] + dirsq[...])
    norm1[...] = alpha1

    def finish(n, c, f, gain):
        del gain
        alpha = row_sum(jnp.where(lane == n, norm1[...], 0.0))
        for part in range(2):
            value = first[n, part] + alpha * second[n, part]
            det[c, pl.ds(part * 512 + f, 16, stride=BAND), :] = value

    def finish_phase(g, _):
        each_inner(g, finish, 5)
        return 0

    lax.fori_loop(0, GROUPS, finish_phase, 0)
    each_edge(finish)

    half = SYM * BAND
    table = jnp.concatenate(
        [
            jnp.concatenate([det[c, pl.ds(0, half), :], det[c, pl.ds(512, half), :]], axis=0).astype(BF16)
            for c in range(2)
        ],
        axis=1,
    )
    for row in range(0, 512, 128):
        slot = lax.broadcasted_iota(jnp.int32, (128, users2), 0) + row
        onehot = jnp.where(slot == place, 1.0, 0.0).astype(BF16)
        sent = lax.dot_general(onehot, table, (((1,), (1,)), ((), ())), preferred_element_type=F32)
        out[pl.ds(row, 128), :] = sent.astype(BF16)


def deliver_kernel(outgoing, arrived, ssem, rsem, lsem):
    c_id, p_id, s_id = lax.axis_index("cell"), lax.axis_index("panel"), lax.axis_index("sc")
    n_sc = lax.axis_size("sc")
    half = n_sc // 2
    barrier = pltpu.get_barrier_semaphore()
    origin = s_id // half

    def panel_to(other):
        return jnp.where(lax.rem(other, 2) == lax.rem(s_id, 2), p_id, 1 - p_id)

    def from_self(j):
        return (origin == c_id) & (j == s_id)

    def to_self(k):
        return (k // half == c_id) & (c_id * half + lax.rem(k, half) == s_id)

    def greet(j, _):
        @pl.when(jnp.logical_not(from_self(j)))
        def _():
            pl.semaphore_signal(barrier, inc=1, device_id=(origin, panel_to(j), j), device_id_type=MESH)

        return 0

    lax.fori_loop(0, n_sc, greet, 0)
    own = origin == c_id
    pl.semaphore_wait(barrier, n_sc - jnp.where(own, 1, 0))

    def target(i):
        k = lax.rem(i + s_id, n_sc)
        return k, c_id * half + lax.rem(k, half)

    def remote(k, other):
        return pltpu.make_async_remote_copy(
            src_ref=outgoing.at[k], dst_ref=arrived.at[s_id], send_sem=ssem.at[k], recv_sem=rsem.at[s_id],
            device_id=(k // half, panel_to(other), other), device_id_type=MESH,
        )

    def local(k):
        return pltpu.make_async_copy(outgoing.at[k], arrived.at[s_id], lsem)

    def send(i, _):
        k, other = target(i)

        @pl.when(to_self(k))
        def _():
            local(k).start()

        @pl.when(jnp.logical_not(to_self(k)))
        def _():
            remote(k, other).start()

        return 0

    lax.fori_loop(0, n_sc, send, 0)

    def finish(i, _):
        k, other = target(i)

        @pl.when(to_self(k))
        def _():
            local(k).wait()

        @pl.when(jnp.logical_not(to_self(k)))
        def _():
            remote(k, other).wait_send()

        @pl.when(jnp.logical_not(from_self(i)))
        def _():
            pltpu.make_async_remote_copy(
                src_ref=outgoing.at[0], dst_ref=arrived.at[i], send_sem=ssem.at[0], recv_sem=rsem.at[i],
                device_id=(origin, panel_to(i), i), device_id_type=MESH,
            ).wait_recv()

        return 0

    lax.fori_loop(0, n_sc, finish, 0)


def assemble_kernel(arrived, out, rows):
    lane = lax.broadcasted_iota(jnp.int32, (16, 128), 1)
    for tile in range(7):
        blocks = [arrived[k, :, pl.ds(128 * tile, 128)].astype(F32) for k in range(4)]
        for m in range(4):
            value = blocks[m]
            for k in range(4):
                if k != m:
                    moved = pltpu.roll(blocks[k], (32 * (k - m)) % 128, 1)
                    inside = (lane >= 32 * k) & (lane < 32 * k + 32)
                    value = jnp.where(inside, moved, value)
            which = 4 * tile + m
            rows[pl.ds((which // SYM) * 16 + which % SYM, 16, stride=32), :] = value
    for slot in range(16):
        for part in range(2):
            out[slot, part] = rows[pl.ds(slot * 32 + part * 16, SYM), :].astype(BF16)


def body(channel, received, noise_power, user_count, serving_cell):
    vmem = pltpu.VMEM
    keys = serving_cell.reshape(2 * USERS, 1).astype(jnp.int32)
    received = jnp.pad(received, ((0, 0), (0, 0), (0, 0), (0, 2), (0, 0)))
    dma = pltpu.SemaphoreType.DMA
    outgoing = pl.pallas_call(
        detect_kernel,
        name="detect",
        out_shape=jax.ShapeDtypeStruct((512, 2 * SYM * BAND), BF16),
        in_specs=[
            pl.BlockSpec(memory_space=pl.ANY),
            pl.BlockSpec(memory_space=pl.ANY),
            pl.BlockSpec(memory_space=pltpu.SMEM),
            pl.BlockSpec(memory_space=pltpu.SMEM),
            pl.BlockSpec(memory_space=vmem),
        ],
        out_specs=pl.BlockSpec(memory_space=vmem),
        scratch_shapes=[
            vmem((2, BAND, 2, ANT, USERS), BF16),
            vmem((UNITS, ANT, 2 * USERS), BF16),
            vmem((2, BAND, 2, 16, ANT), BF16),
            vmem((2, 2, 2, ANT, USERS), BF16),
            vmem((UNITS, 2, 16, USERS), BF16),
            vmem((UNITS, 2, 16, USERS), BF16),
            vmem((UNITS, 2, 16, USERS), BF16),
            vmem((UNITS, 2, 16, USERS), BF16),
            vmem((16, 128), F32),
            vmem((16, 128), F32),
            vmem((16, 128), F32),
            vmem((16, 128), F32),
            vmem((UNITS, 2, 16, USERS), F32),
            vmem((UNITS, 2, 16, USERS), F32),
            vmem((2, 1024, USERS), F32),
            dma((2, PER_CELL + 1)),
            dma((2,)),
            dma((2, 2)),
            dma((2, 2)),
            dma((GROUPS + 1,)),
            dma((GROUPS + 1,)),
            dma((GROUPS + 1,)),
            dma((GROUPS + 1,)),
            dma,
            dma,
        ],
        compiler_params=pltpu.CompilerParams(
            collective_id=0, has_side_effects=True, vmem_limit_bytes=60 * 1024 * 1024
        ),
    )(channel, received, noise_power, user_count, keys)
    arrived = pl.pallas_call(
        deliver_kernel,
        name="deliver",
        out_shape=jax.ShapeDtypeStruct((BAND, 16, 2 * SYM * BAND), BF16),
        in_specs=[pl.BlockSpec(memory_space=pl.ANY)],
        out_specs=pl.BlockSpec(memory_space=pl.ANY),
        scratch_shapes=[dma((32,)), dma((32,)), dma],
        compiler_params=pltpu.CompilerParams(collective_id=1, has_side_effects=True),
    )(outgoing.reshape(32, 16, 2 * SYM * BAND))
    routed = pl.pallas_call(
        assemble_kernel,
        name="assemble",
        grid=(8,),
        out_shape=jax.ShapeDtypeStruct((16, 2, SYM, 32 * BAND), BF16),
        in_specs=[pl.BlockSpec((4, 16, 2 * SYM * BAND), lambda i: (i, 0, 0))],
        out_specs=pl.BlockSpec((16, 2, SYM, 128), lambda i: (0, 0, 0, i)),
        scratch_shapes=[vmem((512, 128), F32)],
    )(arrived)
    return routed.reshape(2, 8, 2, SYM, 32 * BAND)


def solution(mesh):
    return jax.shard_map(
        body,
        mesh=mesh,
        in_specs=(
            P("cell", "sc", None, "panel", None),
            P("cell", "sc", None, None, "panel"),
            P("cell"),
            P("cell", "sc"),
            P("cell", None, None),
        ),
        out_specs=P("cell", "sc", None, None, None),
        check_vma=False,
    )
```

```python
import functools

import jax
import jax.numpy as jnp
from jax import lax
from jax.experimental import pallas as pl
from jax.experimental.pallas import tpu as pltpu
from jax.sharding import PartitionSpec as P

GRP = 16
MESH = pl.DeviceIdType.MESH
F32, BF16 = jnp.float32, jnp.bfloat16

BAND, ANT, USERS, SYM = 32, 512, 128, 14
INNER = BAND - 2
SIZE = 10
PER_CELL = INNER // SIZE
GROUPS = 2 * PER_CELL
UNITS = 2 * BAND


def adjoint(rows, block):
    out = jnp.dot(rows, block, preferred_element_type=F32)
    real = out[:16, :128] + out[16:, 128:]
    imag = out[16:, :128] - out[:16, 128:]
    return real, imag


def forward(real, imag, block):
    left = jnp.concatenate(
        [jnp.concatenate([real, -imag], axis=1), jnp.concatenate([imag, real], axis=1)], axis=0
    )
    return lax.dot_general(left, block, (((1,), (1,)), ((), ())), preferred_element_type=F32)


def row_sum(values):
    return jnp.sum(values, axis=1, keepdims=True)


def detect_kernel(
    channel, received, noise, counts, keys, out,
    raw, smooth, rx, rx_other, split, halo, msend, mrecv, isend, irecv, xsend, xrecv, ysend, yrecv, own2,
    columns, qsend, qrecv, alphas, norm1, dirsq, first, second, det, onehot,
    raw_sem, rx_sem, halo_ssem, halo_rsem, o_ssem, o_rsem, m_ssem, m_rsem, i_ssem, i_rsem,
    x_ssem, x_rsem, q_ssem, q_rsem,
):
    c_id, p_id, s_id = lax.axis_index("cell"), lax.axis_index("panel"), lax.axis_index("sc")
    n_sc = lax.axis_size("sc")
    partner = (c_id, 1 - p_id, s_id)
    upper = (c_id, 1 - p_id, lax.rem(s_id + 1, n_sc))
    lower = (c_id, 1 - p_id, lax.rem(s_id + n_sc - 1, n_sc))
    edges = [(c, side, GROUPS * SIZE + 2 * c + side, side * (BAND - 1)) for c in range(2) for side in range(2)]

    def raw_copy(c, k):
        rows = pl.ds(k * SIZE + 2, SIZE)
        return pltpu.make_async_copy(channel.at[c, rows], raw.at[c, rows], raw_sem.at[c, k])

    def head_copy(c):
        rows = pl.ds(0, 2)
        return pltpu.make_async_copy(channel.at[c, rows], raw.at[c, rows], raw_sem.at[c, PER_CELL])

    def rx_copy(c):
        return pltpu.make_async_copy(received.at[c], rx.at[c, :, pl.ds(0, SYM)], rx_sem.at[c])

    for c in range(2):
        head_copy(c).start()
        rx_copy(c).start()
        for k in range(PER_CELL):
            raw_copy(c, k).start()

    barrier = pltpu.get_barrier_semaphore()
    for device in (partner, upper, lower):
        pl.semaphore_signal(barrier, inc=1, device_id=device, device_id_type=MESH)
    pl.semaphore_wait(barrier, 3)

    def remote(source, target, ssem, rsem, device):
        return pltpu.make_async_remote_copy(
            src_ref=source, dst_ref=target, send_sem=ssem, recv_sem=rsem,
            device_id=device, device_id_type=MESH,
        )

    other_copies = [
        remote(
            received.at[c, f], rx_other.at[c, side, pl.ds(0, SYM)],
            o_ssem.at[c, side], o_rsem.at[c, side], partner,
        )
        for c, side, n, f in edges
    ]
    halo_copies = [
        remote(
            channel.at[c, BAND - 1 - f, part], halo.at[c, side, :, pl.ds(128 * part, 128)],
            halo_ssem.at[c, side, part], halo_rsem.at[c, side, part], (upper, lower)[side],
        )
        for c, side, n, f in edges
        for part in range(2)
    ]
    for copy in halo_copies + other_copies:
        copy.start()

    def group_copy(pair, g):
        source, target, ssem, rsem = pair
        rows = pl.ds(g * SIZE, SIZE)
        return remote(source.at[rows], target.at[rows], ssem.at[g], rsem.at[g], partner)

    def edge_copy(pair):
        source, target, ssem, rsem = pair
        rows = pl.ds(GROUPS * SIZE, 4)
        return remote(source.at[rows], target.at[rows], ssem.at[GROUPS], rsem.at[GROUPS], partner)

    m_pair = (msend, mrecv, m_ssem, m_rsem)
    i_pair = (isend, irecv, i_ssem, i_rsem)
    x_copy = remote(xsend, xrecv, x_ssem.at[0], x_rsem.at[0], partner)
    y_copy = remote(ysend, yrecv, x_ssem.at[1], x_rsem.at[1], partner)
    lane = lax.broadcasted_iota(jnp.int32, (16, 128), 1)

    users2 = 2 * USERS
    key_row = jnp.concatenate([keys[0], keys[1]], axis=1).astype(F32)
    rows_i = lax.broadcasted_iota(jnp.int32, (users2, users2), 0)
    cols_i = lax.broadcasted_iota(jnp.int32, (users2, users2), 1)
    key_f = jnp.sum(jnp.where(rows_i == cols_i, key_row, 0.0), axis=1, keepdims=True)
    earlier = (key_f == key_row) & (rows_i < cols_i)
    rank_row = jnp.sum(jnp.where(earlier, 1.0, 0.0), axis=0, keepdims=True).astype(jnp.int32)
    key_row = key_row.astype(jnp.int32)
    place = (key_row // 2) * 256 + (rank_row // 8) * 16 + lax.rem(key_row, 2) * 8 + lax.rem(rank_row, 8)
    for row in range(0, 512, 64):
        slot = lax.broadcasted_iota(jnp.int32, (64, users2), 0) + row
        onehot[pl.ds(row, 64), :] = jnp.where(slot == place, 1.0, 0.0).astype(BF16)

    def spot(n):
        c = n // INNER
        return c, lax.rem(n, INNER) + 1

    def keep(values, c, f):
        mask = lane < counts[c, f // GRP]
        return [jnp.where(mask, v, 0.0) for v in values]

    def total(mine, theirs, n):
        pad = jnp.zeros((2, USERS), F32)
        return [
            jnp.concatenate([mine[n, a].astype(F32) + theirs[n, a].astype(F32), pad], axis=0)
            for a in range(2)
        ]

    def put(target, n, values, gain):
        for a in range(2):
            target[n, a] = (values[a][:SYM] * gain).astype(BF16)

    def sample_rows(block, k):
        both = block.reshape(32, ANT).astype(F32)
        for tile in range(ANT // 128):
            split[k, tile] = both[:, 128 * tile : 128 * tile + 128]
        return jnp.concatenate(
            [
                jnp.concatenate(
                    [split.at[k, tile][pl.ds(a, 16, stride=2), :] for tile in range(ANT // 128)], axis=1
                )
                for a in range(2)
            ],
            axis=0,
        ).astype(BF16)

    for c in range(2):
        head_copy(c).wait()
        rx_copy(c).wait()

    def first_phase(g, _):
        raw_copy(g // PER_CELL, lax.rem(g, PER_CELL)).wait()
        c = g // PER_CELL
        base = lax.rem(g, PER_CELL) * SIZE

        def strip(i, _):
            rows = pl.ds(pl.multiple_of(i * 32, 32), 32)
            for part in range(2):
                low, here = raw[c, base, part, rows, :], raw[c, base + 1, part, rows, :]
                for j in range(SIZE):
                    high = raw[c, base + j + 2, part, rows, :]
                    smooth[g * SIZE + j, rows, pl.ds(128 * part, 128)] = (low + high) + (here + here)
                    low, here = here, high
            return 0

        lax.fori_loop(0, ANT // 32, strip, 0)

        def match(i, _):
            for k in range(5):
                n = g * SIZE + 5 * i + k
                terms = adjoint(sample_rows(rx[c, base + 5 * i + k + 1], k), smooth[n])
                put(msend, n, terms, 0.25)
            return 0

        lax.fori_loop(0, SIZE // 5, match, 0)
        group_copy(m_pair, g).start()
        return 0

    lax.fori_loop(0, GROUPS, first_phase, 0)

    def edge_strip(i, _):
        rows = pl.ds(pl.multiple_of(i * 64, 64), 64)
        for c, side, n, f in edges:
            for part in range(2):
                here, inner = raw[c, f, part, rows, :], raw[c, 1 + side * (BAND - 3), part, rows, :]
                smooth[n, rows, pl.ds(128 * part, 128)] = inner + (here + here)
        return 0

    lax.fori_loop(0, ANT // 64, edge_strip, 0)

    def pipeline(low, high, begin, stage_a, stage_b, end):
        begin(low)
        stage_a(2 * low, 0)

        def step(g, _):
            stage_b(2 * g, 0)
            stage_a(2 * g + 1, 1)
            begin(g + 1)
            stage_b(2 * g + 1, 1)
            stage_a(2 * g + 2, 0)
            end(g)
            return 0

        lax.fori_loop(low, high - 1, step, 0)
        last = high - 1
        stage_b(2 * last, 0)
        stage_a(2 * last + 1, 1)
        stage_b(2 * last + 1, 1)
        end(last)

    def column_stage(batch, slot):
        for k in range(5):
            n = 5 * batch + k
            real, imag = keep(total(msend, mrecv, n), *spot(n))
            column = forward(real.astype(BF16), imag.astype(BF16), smooth[n])
            columns[slot, k] = (column * 0.25).astype(BF16)

    def image_stage(batch, slot):
        for k in range(5):
            n = 5 * batch + k
            put(isend, n, adjoint(columns[slot, k], smooth[n]), 0.25)

    def image_phase(low, high):
        pipeline(
            low, high, lambda g: group_copy(m_pair, g).wait(), column_stage, image_stage,
            lambda g: group_copy(i_pair, g).start(),
        )

    def step_terms(n, c, f):
        power = noise[c]
        br, bi = keep(total(msend, mrecv, n), c, f)
        ir, ii = keep(total(isend, irecv, n), c, f)
        ir, ii = ir + power * br, ii + power * bi
        norm0 = row_sum(br * br + bi * bi)
        alpha = norm0 / row_sum(br * ir + bi * ii)
        first[n, 0], first[n, 1] = alpha * br, alpha * bi
        rr, ri = br - alpha * ir, bi - alpha * ii
        norm = row_sum(rr * rr + ri * ri)
        beta = norm / norm0
        dr, di = rr + beta * br, ri + beta * bi
        second[n, 0], second[n, 1] = dr, di
        return norm, power * row_sum(dr * dr + di * di)

    def collect(target, pairs):
        value = target[...]
        for n, item in pairs:
            value = jnp.where(lane == n, item, value)
        target[...] = value

    def update_stage(batch, slot):
        del slot
        terms = [(n, step_terms(n, *spot(n))) for n in (5 * batch + k for k in range(5))]
        collect(norm1, [(n, t[0]) for n, t in terms])
        collect(dirsq, [(n, t[1]) for n, t in terms])

    def square_sum(column):
        square = column * column
        square = square[:16] + square[16:]
        return row_sum((square[:, :128] + square[:, 128:256]) + (square[:, 256:384] + square[:, 384:]))

    def norm_stage(batch, slot):
        del slot
        pairs = []
        for k in range(5):
            n = 5 * batch + k
            column = forward(second[n, 0].astype(BF16), second[n, 1].astype(BF16), smooth[n]) * 0.25
            pairs.append((n, square_sum(column)))
        collect(qsend.at[0], pairs)

    def update_phase(low, high):
        pipeline(
            low, high, lambda g: group_copy(i_pair, g).wait(), update_stage, norm_stage, lambda g: None
        )

    ends = (s_id == 0, s_id == n_sc - 1)
    gains = [jnp.where(end, 1.0 / 3.0, 0.25).astype(F32) for end in ends]
    halo_gains = [jnp.where(end, 0.0, 0.25).astype(F32) for end in ends]

    def edge_matched():
        for copy in halo_copies + other_copies:
            copy.wait()
        for c, side, n, f in edges:
            mine = adjoint(sample_rows(rx[c, f], 0), smooth[n])
            theirs = adjoint(sample_rows(rx_other[c, side], 1), halo[c, side])
            put(msend, n, [u * gains[side] + v * halo_gains[side] for u, v in zip(mine, theirs)], 1.0)
        edge_copy(m_pair).start()

    def edge_columns():
        edge_copy(m_pair).wait()
        for e, (c, side, n, f) in enumerate(edges):
            real, imag = [v.astype(BF16) for v in keep(total(msend, mrecv, n), c, f)]
            xsend[0, e] = (forward(real, imag, smooth[n]) * gains[side]).astype(BF16)
            xsend[1, e] = (forward(real, imag, halo[c, side]) * halo_gains[side]).astype(BF16)
        x_copy.start()

    def edge_image():
        x_copy.wait()
        for e, (c, side, n, f) in enumerate(edges):
            mine = (xsend[0, e].astype(F32) + xrecv[1, e].astype(F32)).astype(BF16)
            theirs = (xrecv[0, e].astype(F32) + xsend[1, e].astype(F32)).astype(BF16)
            mine, theirs = adjoint(mine, smooth[n]), adjoint(theirs, halo[c, side])
            put(isend, n, [u * gains[side] + v * halo_gains[side] for u, v in zip(mine, theirs)], 1.0)
        edge_copy(i_pair).start()

    def edge_update():
        edge_copy(i_pair).wait()
        terms = [(n, step_terms(n, c, f)) for c, side, n, f in edges]
        collect(norm1, [(n, t[0]) for n, t in terms])
        collect(dirsq, [(n, t[1]) for n, t in terms])
        for e, (c, side, n, f) in enumerate(edges):
            real, imag = second[n, 0].astype(BF16), second[n, 1].astype(BF16)
            ysend[e] = (forward(real, imag, halo[c, side]) * halo_gains[side]).astype(BF16)
            own2[e] = forward(real, imag, smooth[n]) * gains[side]
        y_copy.start()

    def edge_norm():
        y_copy.wait()
        collect(
            qsend.at[1],
            [(n, square_sum(own2[e] + yrecv[e].astype(F32))) for e, (c, side, n, f) in enumerate(edges)],
        )

    def q_copy(k):
        return remote(qsend.at[k], qrecv.at[k], q_ssem.at[k], q_rsem.at[k], partner)

    qsend[...] = jnp.zeros_like(qsend)
    norm1[...] = jnp.ones_like(norm1)
    dirsq[...] = jnp.ones_like(dirsq)

    image_phase(0, 4)
    edge_matched()
    image_phase(4, GROUPS)
    edge_columns()
    update_phase(0, 2)
    edge_image()
    update_phase(2, 4)
    edge_update()
    update_phase(4, GROUPS)
    q_copy(0).start()
    edge_norm()
    q_copy(1).start()

    def finish(n, c, f):
        alpha = row_sum(jnp.where(lane == n, alphas[n // (GROUPS * SIZE)], 0.0))
        for part in range(2):
            value = first[n, part] + alpha * second[n, part]
            for h in range(2):
                det[c, pl.ds((2 * part + h) * 256 + f * 8, 8), :] = value[8 * h : 8 * h + 8]

    def step_sizes(k):
        q_copy(k).wait()
        alphas[k] = norm1[...] / (qsend[k] + qrecv[k] + dirsq[...])

    def finish_phase(batch, _):
        for k in range(5):
            n = 5 * batch + k
            finish(n, *spot(n))
        return 0

    step_sizes(0)
    lax.fori_loop(0, 2 * GROUPS, finish_phase, 0)
    step_sizes(1)
    for c, side, n, f in edges:
        finish(n, c, f)

    def placed(which, c):
        a, s = which // SYM, which % SYM
        return det[c, pl.ds((2 * a + s // 8) * 256 + s % 8, BAND, stride=8), :].astype(BF16)

    for low in range(0, 2 * SYM, 8):
        high = min(low + 8, 2 * SYM)
        table = jnp.concatenate(
            [jnp.concatenate([placed(w, c) for w in range(low, high)], axis=0) for c in range(2)], axis=1
        )
        sent = lax.dot_general(
            onehot[...], table, (((1,), (1,)), ((), ())), preferred_element_type=F32
        )
        out[:, pl.ds(low * BAND, (high - low) * BAND)] = sent.astype(BF16)


def deliver_kernel(outgoing, arrived, ssem, rsem, lsem):
    c_id, p_id, s_id = lax.axis_index("cell"), lax.axis_index("panel"), lax.axis_index("sc")
    n_sc = lax.axis_size("sc")
    half = n_sc // 2
    barrier = pltpu.get_barrier_semaphore()
    origin = s_id // half

    def panel_to(other):
        return jnp.where(lax.rem(other, 2) == lax.rem(s_id, 2), p_id, 1 - p_id)

    def from_self(j):
        return (origin == c_id) & (j == s_id)

    def to_self(k):
        return (k // half == c_id) & (c_id * half + lax.rem(k, half) == s_id)

    def greet(j, _):
        @pl.when(jnp.logical_not(from_self(j)))
        def _():
            pl.semaphore_signal(barrier, inc=1, device_id=(origin, panel_to(j), j), device_id_type=MESH)

        return 0

    lax.fori_loop(0, n_sc, greet, 0)
    own = origin == c_id
    pl.semaphore_wait(barrier, n_sc - jnp.where(own, 1, 0))

    def target(i):
        k = lax.rem(i + s_id, n_sc)
        return k, c_id * half + lax.rem(k, half)

    def remote(k, other):
        return pltpu.make_async_remote_copy(
            src_ref=outgoing.at[k], dst_ref=arrived.at[s_id], send_sem=ssem.at[k], recv_sem=rsem.at[s_id],
            device_id=(k // half, panel_to(other), other), device_id_type=MESH,
        )

    def local(k):
        return pltpu.make_async_copy(outgoing.at[k], arrived.at[s_id], lsem)

    def send(i, _):
        k, other = target(i)

        @pl.when(to_self(k))
        def _():
            local(k).start()

        @pl.when(jnp.logical_not(to_self(k)))
        def _():
            remote(k, other).start()

        return 0

    lax.fori_loop(0, n_sc, send, 0)

    def finish(i, _):
        k, other = target(i)

        @pl.when(to_self(k))
        def _():
            local(k).wait()

        @pl.when(jnp.logical_not(to_self(k)))
        def _():
            remote(k, other).wait_send()

        @pl.when(jnp.logical_not(from_self(i)))
        def _():
            pltpu.make_async_remote_copy(
                src_ref=outgoing.at[0], dst_ref=arrived.at[i], send_sem=ssem.at[0], recv_sem=rsem.at[i],
                device_id=(origin, panel_to(i), i), device_id_type=MESH,
            ).wait_recv()

        return 0

    lax.fori_loop(0, n_sc, finish, 0)


ROWS = 2 * SYM * 16


def assemble_kernel(arrived, out, mixed, order):
    @pl.when(pl.program_id(0) == 0)
    def _():
        to = lax.broadcasted_iota(jnp.int32, (ROWS, ROWS), 0)
        source = lax.broadcasted_iota(jnp.int32, (ROWS, ROWS), 1)
        which, slot = source // 16, lax.rem(source, 16)
        goes = slot * (2 * SYM) + lax.rem(which, SYM) * 2 + which // SYM
        order[...] = jnp.where(to == goes, 1.0, 0.0).astype(BF16)

    lane = lax.broadcasted_iota(jnp.int32, (16, 128), 1)
    for half in range(2):
        for tile in range(7):
            blocks = [arrived[4 * half + k, :, pl.ds(128 * tile, 128)].astype(F32) for k in range(4)]
            for m in range(4):
                value = blocks[m]
                for k in range(4):
                    if k != m:
                        moved = pltpu.roll(blocks[k], (32 * (k - m)) % 128, 1)
                        inside = (lane >= 32 * k) & (lane < 32 * k + 32)
                        value = jnp.where(inside, moved, value)
                mixed[pl.ds((4 * tile + m) * 16, 16), pl.ds(128 * half, 128)] = value.astype(BF16)
    moved = jnp.dot(order[...], mixed[...], preferred_element_type=F32)
    for slot in range(16):
        rows = moved[slot * 2 * SYM : (slot + 1) * 2 * SYM]
        out[slot] = rows.astype(BF16).reshape(SYM, 2, 256)


def body(channel, received, noise_power, user_count, serving_cell):
    vmem = pltpu.VMEM
    keys = serving_cell.transpose(0, 2, 1)
    received = received.transpose(0, 1, 3, 2, 4)
    dma = pltpu.SemaphoreType.DMA
    outgoing = pl.pallas_call(
        detect_kernel,
        name="detect",
        out_shape=jax.ShapeDtypeStruct((512, 2 * SYM * BAND), BF16),
        in_specs=[
            pl.BlockSpec(memory_space=pl.ANY),
            pl.BlockSpec(memory_space=pl.ANY),
            pl.BlockSpec(memory_space=pltpu.SMEM),
            pl.BlockSpec(memory_space=pltpu.SMEM),
            pl.BlockSpec(memory_space=vmem),
        ],
        out_specs=pl.BlockSpec(memory_space=vmem),
        scratch_shapes=[
            vmem((2, BAND, 2, ANT, USERS), BF16),
            vmem((UNITS, ANT, 2 * USERS), BF16),
            vmem((2, BAND, 16, 2, ANT), BF16),
            vmem((2, 2, 16, 2, ANT), BF16),
            vmem((5, ANT // 128, 32, 128), F32),
            vmem((2, 2, ANT, 2 * USERS), BF16),
            vmem((UNITS, 2, SYM, USERS), BF16),
            vmem((UNITS, 2, SYM, USERS), BF16),
            vmem((UNITS, 2, SYM, USERS), BF16),
            vmem((UNITS, 2, SYM, USERS), BF16),
            vmem((2, 4, 32, ANT), BF16),
            vmem((2, 4, 32, ANT), BF16),
            vmem((4, 32, ANT), BF16),
            vmem((4, 32, ANT), BF16),
            vmem((4, 32, ANT), F32),
            vmem((2, 5, 32, ANT), BF16),
            vmem((2, 16, 128), F32),
            vmem((2, 16, 128), F32),
            vmem((2, 16, 128), F32),
            vmem((16, 128), F32),
            vmem((16, 128), F32),
            vmem((UNITS, 2, 16, USERS), F32),
            vmem((UNITS, 2, 16, USERS), F32),
            vmem((2, 1024, USERS), F32),
            vmem((512, 2 * USERS), BF16),
            dma((2, PER_CELL + 1)),
            dma((2,)),
            dma((2, 2, 2)),
            dma((2, 2, 2)),
            dma((2, 2)),
            dma((2, 2)),
            dma((GROUPS + 1,)),
            dma((GROUPS + 1,)),
            dma((GROUPS + 1,)),
            dma((GROUPS + 1,)),
            dma((2,)),
            dma((2,)),
            dma((2,)),
            dma((2,)),
        ],
        compiler_params=pltpu.CompilerParams(
            collective_id=0, has_side_effects=True, vmem_limit_bytes=60 * 1024 * 1024
        ),
    )(channel, received, noise_power, user_count, keys)
    arrived = pl.pallas_call(
        deliver_kernel,
        name="deliver",
        out_shape=jax.ShapeDtypeStruct((BAND, 16, 2 * SYM * BAND), BF16),
        in_specs=[pl.BlockSpec(memory_space=pl.ANY)],
        out_specs=pl.BlockSpec(memory_space=pl.ANY),
        scratch_shapes=[dma((32,)), dma((32,)), dma],
        compiler_params=pltpu.CompilerParams(collective_id=1, has_side_effects=True),
    )(outgoing.reshape(32, 16, 2 * SYM * BAND))
    routed = pl.pallas_call(
        assemble_kernel,
        name="assemble",
        grid=(4,),
        out_shape=jax.ShapeDtypeStruct((16, SYM, 2, 32 * BAND), BF16),
        in_specs=[pl.BlockSpec((8, 16, 2 * SYM * BAND), lambda i: (i, 0, 0))],
        out_specs=pl.BlockSpec((16, SYM, 2, 256), lambda i: (0, 0, 0, i)),
        scratch_shapes=[vmem((ROWS, 256), BF16), vmem((ROWS, ROWS), BF16)],
    )(arrived)
    return routed.reshape(2, 8, SYM, 2, 32 * BAND).transpose(0, 1, 3, 2, 4)


def solution(mesh):
    return jax.shard_map(
        body,
        mesh=mesh,
        in_specs=(
            P("cell", "sc", None, "panel", None),
            P("cell", "sc", None, None, "panel"),
            P("cell"),
            P("cell", "sc"),
            P("cell", None, None),
        ),
        out_specs=P("cell", "sc", None, None, None),
        check_vma=False,
    )
```

```python
import functools

import jax
import jax.numpy as jnp
from jax import lax
from jax.experimental import pallas as pl
from jax.experimental.pallas import tpu as pltpu
from jax.sharding import PartitionSpec as P

GRP = 16
MESH = pl.DeviceIdType.MESH
F32, BF16 = jnp.float32, jnp.bfloat16

BAND, ANT, USERS, SYM = 32, 512, 128, 14
INNER = BAND - 2
SIZE = 10
PER_CELL = INNER // SIZE
GROUPS = 2 * PER_CELL
UNITS = 2 * BAND


def combine(out):
    return out[:16, :128] + out[16:, 128:], out[16:, :128] - out[:16, 128:]


def adjoint(rows, block):
    return combine(jnp.dot(rows, block, preferred_element_type=F32))


def forward(real, imag, block):
    left = jnp.concatenate(
        [jnp.concatenate([real, -imag], axis=1), jnp.concatenate([imag, real], axis=1)], axis=0
    )
    return lax.dot_general(left, block, (((1,), (1,)), ((), ())), preferred_element_type=F32)


def row_sum(values):
    return jnp.sum(values, axis=1, keepdims=True)


def detect_kernel(
    channel, received, noise, counts, keys, arrived,
    raw, smooth, gram, edge, rx, rx_other, split, halo, msend, mrecv, isend, irecv, xsend, xrecv, ysend, yrecv,
    qsend, qrecv, alphas, norm1, dirsq, first, second, det, onehot, outgoing,
    raw_sem, rx_sem, halo_ssem, halo_rsem, o_ssem, o_rsem, m_ssem, m_rsem, i_ssem, i_rsem,
    x_ssem, x_rsem, q_ssem, q_rsem, d_ssem, d_rsem, d_lsem,
):
    c_id, p_id, s_id = lax.axis_index("cell"), lax.axis_index("panel"), lax.axis_index("sc")
    n_sc = lax.axis_size("sc")
    partner = (c_id, 1 - p_id, s_id)
    upper = (c_id, 1 - p_id, lax.rem(s_id + 1, n_sc))
    lower = (c_id, 1 - p_id, lax.rem(s_id + n_sc - 1, n_sc))
    edges = [(c, side, GROUPS * SIZE + 2 * c + side, side * (BAND - 1)) for c in range(2) for side in range(2)]

    def raw_copy(c, k):
        rows = pl.ds(k * SIZE + 2, SIZE)
        return pltpu.make_async_copy(channel.at[c, rows], raw.at[c, rows], raw_sem.at[c, k])

    def head_copy(c):
        rows = pl.ds(0, 2)
        return pltpu.make_async_copy(channel.at[c, rows], raw.at[c, rows], raw_sem.at[c, PER_CELL])

    def rx_copy(c):
        return pltpu.make_async_copy(received.at[c], rx.at[c, :, pl.ds(0, SYM)], rx_sem.at[c])

    for c in range(2):
        head_copy(c).start()
        rx_copy(c).start()
        for k in range(PER_CELL):
            raw_copy(c, k).start()

    barrier = pltpu.get_barrier_semaphore()
    for device in (partner, upper, lower):
        pl.semaphore_signal(barrier, inc=1, device_id=device, device_id_type=MESH)

    half = n_sc // 2
    origin = s_id // half

    def panel_to(other):
        return jnp.where(lax.rem(other, 2) == lax.rem(s_id, 2), p_id, 1 - p_id)

    def from_self(j):
        return (origin == c_id) & (j == s_id)

    def greet(j, _):
        @pl.when(jnp.logical_not(from_self(j)))
        def _():
            pl.semaphore_signal(barrier, inc=1, device_id=(origin, panel_to(j), j), device_id_type=MESH)

        return 0

    lax.fori_loop(0, n_sc, greet, 0)
    pl.semaphore_wait(barrier, 3 + n_sc - jnp.where(origin == c_id, 1, 0))

    def remote(source, target, ssem, rsem, device):
        return pltpu.make_async_remote_copy(
            src_ref=source, dst_ref=target, send_sem=ssem, recv_sem=rsem,
            device_id=device, device_id_type=MESH,
        )

    other_copies = [
        remote(
            received.at[c, f], rx_other.at[c, side, pl.ds(0, SYM)],
            o_ssem.at[c, side], o_rsem.at[c, side], partner,
        )
        for c, side, n, f in edges
    ]
    halo_copies = [
        remote(
            channel.at[c, BAND - 1 - f, part], halo.at[c, side, :, pl.ds(128 * part, 128)],
            halo_ssem.at[c, side, part], halo_rsem.at[c, side, part], (upper, lower)[side],
        )
        for c, side, n, f in edges
        for part in range(2)
    ]
    for copy in halo_copies + other_copies:
        copy.start()

    def group_copy(pair, g):
        source, target, ssem, rsem = pair
        rows = pl.ds(g * SIZE, SIZE)
        return remote(source.at[rows], target.at[rows], ssem.at[g], rsem.at[g], partner)

    def edge_copy(pair, c):
        source, target, ssem, rsem = pair
        rows = pl.ds(GROUPS * SIZE + 2 * c, 2)
        return remote(source.at[rows], target.at[rows], ssem.at[GROUPS + c], rsem.at[GROUPS + c], partner)

    m_pair = (msend, mrecv, m_ssem, m_rsem)
    i_pair = (isend, irecv, i_ssem, i_rsem)

    def x_copy(c):
        return remote(xsend.at[c], xrecv.at[c], x_ssem.at[0, c], x_rsem.at[0, c], partner)

    def y_copy(c):
        return remote(ysend.at[c], yrecv.at[c], x_ssem.at[1, c], x_rsem.at[1, c], partner)

    lane = lax.broadcasted_iota(jnp.int32, (16, 128), 1)

    users2 = 2 * USERS
    key_row = jnp.concatenate([keys[0], keys[1]], axis=1).astype(F32)
    rows_i = lax.broadcasted_iota(jnp.int32, (users2, users2), 0)
    cols_i = lax.broadcasted_iota(jnp.int32, (users2, users2), 1)
    key_f = jnp.sum(jnp.where(rows_i == cols_i, key_row, 0.0), axis=1, keepdims=True)
    earlier = (key_f == key_row) & (rows_i < cols_i)
    rank_row = jnp.sum(jnp.where(earlier, 1.0, 0.0), axis=0, keepdims=True).astype(jnp.int32)
    key_row = key_row.astype(jnp.int32)
    place = (key_row // 2) * 256 + (rank_row // 8) * 16 + lax.rem(key_row, 2) * 8 + lax.rem(rank_row, 8)
    for row in range(0, 512, 64):
        slot = lax.broadcasted_iota(jnp.int32, (64, users2), 0) + row
        onehot[pl.ds(row, 64), :] = jnp.where(slot == place, 1.0, 0.0).astype(BF16)

    def spot(n):
        c = n // INNER
        return c, lax.rem(n, INNER) + 1

    def keep(values, c, f):
        mask = lane < counts[c, f // GRP]
        return [jnp.where(mask, v, 0.0) for v in values]

    def total(mine, theirs, n):
        pad = jnp.zeros((2, USERS), F32)
        return [
            jnp.concatenate([mine[n, a].astype(F32) + theirs[n, a].astype(F32), pad], axis=0)
            for a in range(2)
        ]

    def put(target, n, values, gain):
        for a in range(2):
            target[n, a] = (values[a][:SYM] * gain).astype(BF16)

    def sample_rows(block, k):
        both = block.reshape(32, ANT).astype(F32)
        for tile in range(ANT // 128):
            split[k, tile] = both[:, 128 * tile : 128 * tile + 128]
        return jnp.concatenate(
            [
                jnp.concatenate(
                    [split.at[k, tile][pl.ds(a, 16, stride=2), :] for tile in range(ANT // 128)], axis=1
                )
                for a in range(2)
            ],
            axis=0,
        ).astype(BF16)

    for c in range(2):
        head_copy(c).wait()
        rx_copy(c).wait()

    def smooth_stage(batch, slot):
        c, base = batch // (2 * PER_CELL), lax.rem(batch, 2 * PER_CELL) * 5
        for part in range(2):
            for row in range(0, ANT, 32):
                rows = pl.ds(row, 32)
                low, here = raw[c, base, part, rows, :], raw[c, base + 1, part, rows, :]
                for k in range(5):
                    high = raw[c, base + k + 2, part, rows, :]
                    smooth[slot, k, rows, pl.ds(128 * part, 128)] = (low + high) + (here + here)
                    low, here = here, high

    def gram_stage(batch, slot):
        for k in range(5):
            n = 5 * batch + k
            c, f = spot(n)
            block = smooth[slot, k]
            left = jnp.concatenate([block.T, sample_rows(rx[c, f], k)], axis=0)
            product = jnp.dot(left, block, preferred_element_type=F32)
            gram[n, pl.ds(0, 128), :] = (product[:128, :128] + product[128:256, 128:]).astype(BF16)
            gram[n, pl.ds(128, 128), :] = (product[:128, 128:] - product[128:256, :128]).astype(BF16)
            put(msend, n, combine(product[256:]), 0.25)

    def gram_apply(n, real, imag):
        real, imag = real.astype(BF16), imag.astype(BF16)
        left = jnp.concatenate(
            [jnp.concatenate([real, imag], axis=1), jnp.concatenate([imag, -real], axis=1)], axis=0
        )
        result = jnp.dot(left, gram[n], preferred_element_type=F32)
        return result[:16], result[16:]

    def image_phase(g):
        group_copy(m_pair, g).wait()

        def step(i, _):
            for k in range(5):
                n = g * SIZE + 5 * i + k
                put(isend, n, gram_apply(n, *keep(total(msend, mrecv, n), *spot(n))), 0.0625)
            return 0

        lax.fori_loop(0, SIZE // 5, step, 0)
        group_copy(i_pair, g).start()

    def step_terms(n, c, f):
        power = noise[c]
        br, bi = keep(total(msend, mrecv, n), c, f)
        ir, ii = keep(total(isend, irecv, n), c, f)
        ir, ii = ir + power * br, ii + power * bi
        norm0 = row_sum(br * br + bi * bi)
        alpha = norm0 / row_sum(br * ir + bi * ii)
        first[n, 0], first[n, 1] = alpha * br, alpha * bi
        rr, ri = br - alpha * ir, bi - alpha * ii
        norm = row_sum(rr * rr + ri * ri)
        beta = norm / norm0
        dr, di = rr + beta * br, ri + beta * bi
        second[n, 0], second[n, 1] = dr, di
        return norm, power * row_sum(dr * dr + di * di), dr, di

    def collect(target, pairs):
        value = target[...]
        for n, item in pairs:
            value = jnp.where(lane == n, item, value)
        target[...] = value

    def update_phase(g):
        group_copy(i_pair, g).wait()

        def step(i, _):
            spots = [g * SIZE + 5 * i + k for k in range(5)]
            terms = [step_terms(n, *spot(n)) for n in spots]
            squares = []
            for n, (_norm, _dirsq, dr, di) in zip(spots, terms):
                gr, gi = gram_apply(n, dr, di)
                squares.append(row_sum(dr * gr + di * gi) * 0.0625)
            collect(norm1, [(n, t[0]) for n, t in zip(spots, terms)])
            collect(dirsq, [(n, t[1]) for n, t in zip(spots, terms)])
            collect(qsend.at[0], list(zip(spots, squares)))
            return 0

        lax.fori_loop(0, SIZE // 5, step, 0)

    def square_sum(column):
        square = column * column
        square = square[:16] + square[16:]
        return row_sum((square[:, :128] + square[:, 128:256]) + (square[:, 256:384] + square[:, 384:]))

    ends = (s_id == 0, s_id == n_sc - 1)
    gains = [jnp.where(end, 1.0 / 3.0, 0.25).astype(F32) for end in ends]
    halo_gains = [jnp.where(end, 0.0, 0.25).astype(F32) for end in ends]

    def own_edges(cell):
        return [(2 * cell + side, side, GROUPS * SIZE + 2 * cell + side, side * (BAND - 1)) for side in range(2)]

    def edge_matched(c):
        for copy in halo_copies[4 * c : 4 * c + 4] + other_copies[2 * c : 2 * c + 2]:
            copy.wait()
        for e, side, n, f in own_edges(c):
            mine = adjoint(sample_rows(rx[c, f], 0), edge[e])
            theirs = adjoint(sample_rows(rx_other[c, side], 1), halo[c, side])
            put(msend, n, [u * gains[side] + v * halo_gains[side] for u, v in zip(mine, theirs)], 1.0)
        edge_copy(m_pair, c).start()

    def edge_products(target, c, real, imag, e, side):
        target[c, 0, side] = (forward(real, imag, edge[e]) * gains[side]).astype(BF16)
        target[c, 1, side] = (forward(real, imag, halo[c, side]) * halo_gains[side]).astype(BF16)

    def edge_sums(sent, got, c, side):
        mine = sent[c, 0, side].astype(F32) + got[c, 1, side].astype(F32)
        theirs = got[c, 0, side].astype(F32) + sent[c, 1, side].astype(F32)
        return mine, theirs

    def edge_columns(c):
        edge_copy(m_pair, c).wait()
        for e, side, n, f in own_edges(c):
            real, imag = [v.astype(BF16) for v in keep(total(msend, mrecv, n), c, f)]
            edge_products(xsend, c, real, imag, e, side)
        x_copy(c).start()

    def edge_image(c):
        x_copy(c).wait()
        for e, side, n, f in own_edges(c):
            mine, theirs = [v.astype(BF16) for v in edge_sums(xsend, xrecv, c, side)]
            mine, theirs = adjoint(mine, edge[e]), adjoint(theirs, halo[c, side])
            put(isend, n, [u * gains[side] + v * halo_gains[side] for u, v in zip(mine, theirs)], 1.0)
        edge_copy(i_pair, c).start()

    def edge_update(c):
        edge_copy(i_pair, c).wait()
        found = own_edges(c)
        terms = [(n, step_terms(n, c, f)) for e, side, n, f in found]
        collect(norm1, [(n, t[0]) for n, t in terms])
        collect(dirsq, [(n, t[1]) for n, t in terms])
        for (e, side, n, f), (_n, t) in zip(found, terms):
            edge_products(ysend, c, t[2].astype(BF16), t[3].astype(BF16), e, side)
        y_copy(c).start()

    def edge_norm(c):
        y_copy(c).wait()
        pairs = []
        for e, side, n, f in own_edges(c):
            mine, theirs = edge_sums(ysend, yrecv, c, side)
            pairs.append((n, square_sum(mine) + square_sum(theirs)))
        collect(qsend.at[1], pairs)

    q_copy = remote(qsend.at[0], qrecv, q_ssem, q_rsem, partner)

    qsend[...] = jnp.zeros_like(qsend)
    norm1[...] = jnp.ones_like(norm1)
    dirsq[...] = jnp.ones_like(dirsq)

    def finish(n, c, f):
        alpha = row_sum(jnp.where(lane == n, alphas[n // (GROUPS * SIZE)], 0.0))
        for part in range(2):
            value = first[n, part] + alpha * second[n, part]
            for h in range(2):
                det[c, pl.ds((2 * part + h) * 256 + f * 8, 8), :] = value[8 * h : 8 * h + 8]

    def step_sizes(k):
        if k == 0:
            q_copy.wait()
        square = qsend[0] + qrecv[...] if k == 0 else qsend[1]
        alphas[k] = norm1[...] / (square + dirsq[...])

    def finish_phase(batch, _):
        for k in range(5):
            n = 5 * batch + k
            finish(n, *spot(n))
        return 0

    def edge_blocks(c):
        def strip(i, _):
            rows = pl.ds(pl.multiple_of(i * 64, 64), 64)
            for e, side, n, f in own_edges(c):
                for part in range(2):
                    here, inner = raw[c, f, part, rows, :], raw[c, 1 + side * (BAND - 3), part, rows, :]
                    edge[e, rows, pl.ds(128 * part, 128)] = inner + (here + here)
            return 0

        lax.fori_loop(0, ANT // 64, strip, 0)

    def raw_wait(g):
        raw_copy(g // PER_CELL, lax.rem(g, PER_CELL)).wait()

    raw_wait(0)
    smooth_stage(0, 0)

    def main_step(g, _):
        gram_stage(2 * g, 0)
        smooth_stage(2 * g + 1, 1)
        raw_wait(g + 1)
        gram_stage(2 * g + 1, 1)
        smooth_stage(2 * g + 2, 0)
        group_copy(m_pair, g).start()

        @pl.when(g >= 1)
        def _():
            image_phase(g - 1)

        @pl.when(g >= 2)
        def _():
            update_phase(g - 2)

        @pl.when(g == 2)
        def _():
            edge_blocks(0)
            edge_matched(0)

        @pl.when(g == 3)
        def _():
            edge_columns(0)

        @pl.when(g == 4)
        def _():
            edge_blocks(1)
            edge_matched(1)
            edge_image(0)

        return 0

    last = GROUPS - 1
    lax.fori_loop(0, last, main_step, 0)
    gram_stage(2 * last, 0)
    smooth_stage(2 * last + 1, 1)
    edge_columns(1)
    gram_stage(2 * last + 1, 1)
    group_copy(m_pair, last).start()
    image_phase(last - 1)
    edge_update(0)
    update_phase(last - 2)
    edge_image(1)
    image_phase(last)
    update_phase(last - 1)
    edge_update(1)
    update_phase(last)
    q_copy.start()
    edge_norm(0)
    edge_norm(1)
    step_sizes(1)
    for c, side, n, f in edges:
        finish(n, c, f)
    step_sizes(0)
    lax.fori_loop(0, 2 * GROUPS, finish_phase, 0)

    def placed(which, c):
        a, s = which // SYM, which % SYM
        return det[c, pl.ds((2 * a + s // 8) * 256 + s % 8, BAND, stride=8), :].astype(BF16)

    for low in range(0, 2 * SYM, 8):
        high = min(low + 8, 2 * SYM)
        table = jnp.concatenate(
            [jnp.concatenate([placed(w, c) for w in range(low, high)], axis=0) for c in range(2)], axis=1
        )
        sent = lax.dot_general(
            onehot[...], table, (((1,), (1,)), ((), ())), preferred_element_type=F32
        )
        sent = sent.astype(BF16).reshape(32, 16, (high - low) * BAND)
        outgoing[:, :, pl.ds(low * BAND, (high - low) * BAND)] = sent

    def target(i):
        k = lax.rem(i + s_id, n_sc)
        return k, c_id * half + lax.rem(k, half)

    def to_self(k):
        return (k // half == c_id) & (c_id * half + lax.rem(k, half) == s_id)

    def parcel(k, other):
        return remote(
            outgoing.at[k], arrived.at[s_id], d_ssem.at[k], d_rsem.at[s_id], (k // half, panel_to(other), other)
        )

    def local_parcel(k):
        return pltpu.make_async_copy(outgoing.at[k], arrived.at[s_id], d_lsem)

    def send(i, _):
        k, other = target(i)

        @pl.when(to_self(k))
        def _():
            local_parcel(k).start()

        @pl.when(jnp.logical_not(to_self(k)))
        def _():
            parcel(k, other).start()

        return 0

    lax.fori_loop(0, n_sc, send, 0)

    def settle(i, _):
        k, other = target(i)

        @pl.when(to_self(k))
        def _():
            local_parcel(k).wait()

        @pl.when(jnp.logical_not(to_self(k)))
        def _():
            parcel(k, other).wait_send()

        @pl.when(jnp.logical_not(from_self(i)))
        def _():
            remote(
                outgoing.at[0], arrived.at[i], d_ssem.at[0], d_rsem.at[i], (origin, panel_to(i), i)
            ).wait_recv()

        return 0

    lax.fori_loop(0, n_sc, settle, 0)


ROWS = 2 * SYM * 16


def assemble_kernel(arrived, out, mixed, order):
    @pl.when(pl.program_id(0) == 0)
    def _():
        to = lax.broadcasted_iota(jnp.int32, (ROWS, ROWS), 0)
        source = lax.broadcasted_iota(jnp.int32, (ROWS, ROWS), 1)
        which, slot = source // 16, lax.rem(source, 16)
        goes = slot * (2 * SYM) + lax.rem(which, SYM) * 2 + which // SYM
        order[...] = jnp.where(to == goes, 1.0, 0.0).astype(BF16)

    lane = lax.broadcasted_iota(jnp.int32, (16, 128), 1)
    for half in range(2):
        for tile in range(7):
            blocks = [arrived[4 * half + k, :, pl.ds(128 * tile, 128)].astype(F32) for k in range(4)]
            for m in range(4):
                value = blocks[m]
                for k in range(4):
                    if k != m:
                        moved = pltpu.roll(blocks[k], (32 * (k - m)) % 128, 1)
                        inside = (lane >= 32 * k) & (lane < 32 * k + 32)
                        value = jnp.where(inside, moved, value)
                mixed[pl.ds((4 * tile + m) * 16, 16), pl.ds(128 * half, 128)] = value.astype(BF16)
    moved = jnp.dot(order[...], mixed[...], preferred_element_type=F32)
    for slot in range(16):
        rows = moved[slot * 2 * SYM : (slot + 1) * 2 * SYM]
        out[slot] = rows.astype(BF16).reshape(SYM, 2, 256)


def body(channel, received, noise_power, user_count, serving_cell):
    vmem = pltpu.VMEM
    keys = serving_cell.transpose(0, 2, 1)
    received = received.transpose(0, 1, 3, 2, 4)
    dma = pltpu.SemaphoreType.DMA
    arrived = pl.pallas_call(
        detect_kernel,
        name="detect",
        out_shape=jax.ShapeDtypeStruct((32, 16, 2 * SYM * BAND), BF16),
        in_specs=[
            pl.BlockSpec(memory_space=pl.ANY),
            pl.BlockSpec(memory_space=pl.ANY),
            pl.BlockSpec(memory_space=pltpu.SMEM),
            pl.BlockSpec(memory_space=pltpu.SMEM),
            pl.BlockSpec(memory_space=vmem),
        ],
        out_specs=pl.BlockSpec(memory_space=pl.ANY),
        scratch_shapes=[
            vmem((2, BAND, 2, ANT, USERS), BF16),
            vmem((2, 5, ANT, 2 * USERS), BF16),
            vmem((GROUPS * SIZE, 2 * USERS, USERS), BF16),
            vmem((4, ANT, 2 * USERS), BF16),
            vmem((2, BAND, 16, 2, ANT), BF16),
            vmem((2, 2, 16, 2, ANT), BF16),
            vmem((5, ANT // 128, 32, 128), F32),
            vmem((2, 2, ANT, 2 * USERS), BF16),
            vmem((UNITS, 2, SYM, USERS), BF16),
            vmem((UNITS, 2, SYM, USERS), BF16),
            vmem((UNITS, 2, SYM, USERS), BF16),
            vmem((UNITS, 2, SYM, USERS), BF16),
            vmem((2, 2, 2, 32, ANT), BF16),
            vmem((2, 2, 2, 32, ANT), BF16),
            vmem((2, 2, 2, 32, ANT), BF16),
            vmem((2, 2, 2, 32, ANT), BF16),
            vmem((2, 16, 128), F32),
            vmem((16, 128), F32),
            vmem((2, 16, 128), F32),
            vmem((16, 128), F32),
            vmem((16, 128), F32),
            vmem((UNITS, 2, 16, USERS), F32),
            vmem((UNITS, 2, 16, USERS), F32),
            vmem((2, 1024, USERS), F32),
            vmem((512, 2 * USERS), BF16),
            vmem((32, 16, 2 * SYM * BAND), BF16),
            dma((2, PER_CELL + 1)),
            dma((2,)),
            dma((2, 2, 2)),
            dma((2, 2, 2)),
            dma((2, 2)),
            dma((2, 2)),
            dma((GROUPS + 2,)),
            dma((GROUPS + 2,)),
            dma((GROUPS + 2,)),
            dma((GROUPS + 2,)),
            dma((2, 2)),
            dma((2, 2)),
            dma,
            dma,
            dma((32,)),
            dma((32,)),
            dma,
        ],
        compiler_params=pltpu.CompilerParams(
            collective_id=0, has_side_effects=True, vmem_limit_bytes=60 * 1024 * 1024
        ),
    )(channel, received, noise_power, user_count, keys)
    routed = pl.pallas_call(
        assemble_kernel,
        name="assemble",
        grid=(4,),
        out_shape=jax.ShapeDtypeStruct((16, SYM, 2, 32 * BAND), BF16),
        in_specs=[pl.BlockSpec((8, 16, 2 * SYM * BAND), lambda i: (i, 0, 0))],
        out_specs=pl.BlockSpec((16, SYM, 2, 256), lambda i: (0, 0, 0, i)),
        scratch_shapes=[vmem((ROWS, 256), BF16), vmem((ROWS, ROWS), BF16)],
    )(arrived)
    return routed.reshape(2, 8, SYM, 2, 32 * BAND).transpose(0, 1, 3, 2, 4)


def solution(mesh):
    return jax.shard_map(
        body,
        mesh=mesh,
        in_specs=(
            P("cell", "sc", None, "panel", None),
            P("cell", "sc", None, None, "panel"),
            P("cell"),
            P("cell", "sc"),
            P("cell", None, None),
        ),
        out_specs=P("cell", "sc", None, None, None),
        check_vma=False,
    )
```

```python
import functools

import jax
import jax.numpy as jnp
from jax import lax
from jax.experimental import pallas as pl
from jax.experimental.pallas import tpu as pltpu
from jax.sharding import PartitionSpec as P

GRP = 16
MESH = pl.DeviceIdType.MESH
F32, BF16 = jnp.float32, jnp.bfloat16

BAND, ANT, USERS, SYM = 32, 512, 128, 14
INNER = BAND - 2
SIZE = 10
PER_CELL = INNER // SIZE
GROUPS = 2 * PER_CELL
UNITS = 2 * BAND


def combine(out):
    return out[:16, :128] + out[16:, 128:], out[16:, :128] - out[:16, 128:]


def adjoint(rows, block):
    return combine(jnp.dot(rows, block, preferred_element_type=F32))


def forward(real, imag, block):
    left = jnp.concatenate(
        [jnp.concatenate([real, -imag], axis=1), jnp.concatenate([imag, real], axis=1)], axis=0
    )
    return lax.dot_general(left, block, (((1,), (1,)), ((), ())), preferred_element_type=F32)


def row_sum(values):
    return jnp.sum(values, axis=1, keepdims=True)


def detect_kernel(
    channel, received, noise, counts, keys, arrived,
    raw, smooth, gram, edge, rx, rx_other, split, halo, msend, mrecv, isend, irecv, xsend, xrecv, ysend, yrecv, own2,
    qsend, qrecv, alphas, norm1, dirsq, first, second, det, onehot, outgoing,
    raw_sem, rx_sem, halo_ssem, halo_rsem, o_ssem, o_rsem, m_ssem, m_rsem, i_ssem, i_rsem,
    x_ssem, x_rsem, q_ssem, q_rsem, d_ssem, d_rsem, d_lsem,
):
    c_id, p_id, s_id = lax.axis_index("cell"), lax.axis_index("panel"), lax.axis_index("sc")
    n_sc = lax.axis_size("sc")
    partner = (c_id, 1 - p_id, s_id)
    upper = (c_id, 1 - p_id, lax.rem(s_id + 1, n_sc))
    lower = (c_id, 1 - p_id, lax.rem(s_id + n_sc - 1, n_sc))
    edges = [(c, side, GROUPS * SIZE + 2 * c + side, side * (BAND - 1)) for c in range(2) for side in range(2)]

    def raw_copy(c, k):
        rows = pl.ds(k * SIZE + 2, SIZE)
        return pltpu.make_async_copy(channel.at[c, rows], raw.at[c, rows], raw_sem.at[c, k])

    def head_copy(c):
        rows = pl.ds(0, 2)
        return pltpu.make_async_copy(channel.at[c, rows], raw.at[c, rows], raw_sem.at[c, PER_CELL])

    def rx_copy(c):
        return pltpu.make_async_copy(received.at[c], rx.at[c, :, pl.ds(0, SYM)], rx_sem.at[c])

    for c in range(2):
        head_copy(c).start()
        rx_copy(c).start()
        for k in range(PER_CELL):
            raw_copy(c, k).start()

    barrier = pltpu.get_barrier_semaphore()
    for device in (partner, upper, lower):
        pl.semaphore_signal(barrier, inc=1, device_id=device, device_id_type=MESH)

    half = n_sc // 2
    origin = s_id // half

    def panel_to(other):
        return jnp.where(lax.rem(other, 2) == lax.rem(s_id, 2), p_id, 1 - p_id)

    def from_self(j):
        return (origin == c_id) & (j == s_id)

    def greet(j, _):
        @pl.when(jnp.logical_not(from_self(j)))
        def _():
            pl.semaphore_signal(barrier, inc=1, device_id=(origin, panel_to(j), j), device_id_type=MESH)

        return 0

    lax.fori_loop(0, n_sc, greet, 0)
    pl.semaphore_wait(barrier, 3 + n_sc - jnp.where(origin == c_id, 1, 0))

    def remote(source, target, ssem, rsem, device):
        return pltpu.make_async_remote_copy(
            src_ref=source, dst_ref=target, send_sem=ssem, recv_sem=rsem,
            device_id=device, device_id_type=MESH,
        )

    other_copies = [
        remote(
            received.at[c, f], rx_other.at[c, side, pl.ds(0, SYM)],
            o_ssem.at[c, side], o_rsem.at[c, side], partner,
        )
        for c, side, n, f in edges
    ]
    halo_copies = [
        remote(
            channel.at[c, BAND - 1 - f, part], halo.at[c, side, :, pl.ds(128 * part, 128)],
            halo_ssem.at[c, side, part], halo_rsem.at[c, side, part], (upper, lower)[side],
        )
        for c, side, n, f in edges
        for part in range(2)
    ]
    for copy in halo_copies + other_copies:
        copy.start()

    def group_copy(pair, g):
        source, target, ssem, rsem = pair
        rows = pl.ds(g * SIZE, SIZE)
        return remote(source.at[rows], target.at[rows], ssem.at[g], rsem.at[g], partner)

    def edge_copy(pair, c):
        source, target, ssem, rsem = pair
        rows = pl.ds(GROUPS * SIZE + 2 * c, 2)
        return remote(source.at[rows], target.at[rows], ssem.at[GROUPS + c], rsem.at[GROUPS + c], partner)

    m_pair = (msend, mrecv, m_ssem, m_rsem)
    i_pair = (isend, irecv, i_ssem, i_rsem)

    def x_copy(c):
        return remote(xsend.at[c], xrecv.at[c], x_ssem.at[0, c], x_rsem.at[0, c], partner)

    def y_copy(c):
        return remote(ysend.at[c], yrecv.at[c], x_ssem.at[1, c], x_rsem.at[1, c], partner)

    lane = lax.broadcasted_iota(jnp.int32, (16, 128), 1)

    users2 = 2 * USERS
    key_row = jnp.concatenate([keys[0], keys[1]], axis=1).astype(F32)
    rows_i = lax.broadcasted_iota(jnp.int32, (users2, users2), 0)
    cols_i = lax.broadcasted_iota(jnp.int32, (users2, users2), 1)
    key_f = jnp.sum(jnp.where(rows_i == cols_i, key_row, 0.0), axis=1, keepdims=True)
    earlier = (key_f == key_row) & (rows_i < cols_i)
    rank_row = jnp.sum(jnp.where(earlier, 1.0, 0.0), axis=0, keepdims=True).astype(jnp.int32)
    key_row = key_row.astype(jnp.int32)
    place = (key_row // 2) * 256 + (rank_row // 8) * 16 + lax.rem(key_row, 2) * 8 + lax.rem(rank_row, 8)
    for row in range(0, 512, 64):
        slot = lax.broadcasted_iota(jnp.int32, (64, users2), 0) + row
        onehot[pl.ds(row, 64), :] = jnp.where(slot == place, 1.0, 0.0).astype(BF16)

    def spot(n):
        c = n // INNER
        return c, lax.rem(n, INNER) + 1

    def keep(values, c, f):
        mask = lane < counts[c, f // GRP]
        return [jnp.where(mask, v, 0.0) for v in values]

    def total(mine, theirs, n):
        pad = jnp.zeros((2, USERS), F32)
        return [
            jnp.concatenate([mine[n, a].astype(F32) + theirs[n, a].astype(F32), pad], axis=0)
            for a in range(2)
        ]

    def put(target, n, values, gain):
        for a in range(2):
            target[n, a] = (values[a][:SYM] * gain).astype(BF16)

    def sample_rows(block, k):
        both = block.reshape(32, ANT).astype(F32)
        for tile in range(ANT // 128):
            split[k, tile] = both[:, 128 * tile : 128 * tile + 128]
        return jnp.concatenate(
            [
                jnp.concatenate(
                    [split.at[k, tile][pl.ds(a, 16, stride=2), :] for tile in range(ANT // 128)], axis=1
                )
                for a in range(2)
            ],
            axis=0,
        ).astype(BF16)

    for c in range(2):
        head_copy(c).wait()
        rx_copy(c).wait()

    def smooth_stage(batch, slot):
        c, base = batch // (2 * PER_CELL), lax.rem(batch, 2 * PER_CELL) * 5
        for part in range(2):
            for row in range(0, ANT, 32):
                rows = pl.ds(row, 32)
                low, here = raw[c, base, part, rows, :], raw[c, base + 1, part, rows, :]
                for k in range(5):
                    high = raw[c, base + k + 2, part, rows, :]
                    smooth[slot, k, rows, pl.ds(128 * part, 128)] = (low + high) + (here + here)
                    low, here = here, high

    def gram_stage(batch, slot):
        for k in range(5):
            n = 5 * batch + k
            c, f = spot(n)
            block = smooth[slot, k]
            left = jnp.concatenate([block.T, sample_rows(rx[c, f], k)], axis=0)
            product = jnp.dot(left, block, preferred_element_type=F32)
            gram[n, pl.ds(0, 128), :] = (product[:128, :128] + product[128:256, 128:]).astype(BF16)
            gram[n, pl.ds(128, 128), :] = (product[:128, 128:] - product[128:256, :128]).astype(BF16)
            put(msend, n, combine(product[256:]), 0.25)

    def gram_apply(n, real, imag):
        real, imag = real.astype(BF16), imag.astype(BF16)
        left = jnp.concatenate(
            [jnp.concatenate([real, imag], axis=1), jnp.concatenate([imag, -real], axis=1)], axis=0
        )
        result = jnp.dot(left, gram[n], preferred_element_type=F32)
        return result[:16], result[16:]

    def image_phase(g):
        group_copy(m_pair, g).wait()

        def step(i, _):
            for k in range(5):
                n = g * SIZE + 5 * i + k
                put(isend, n, gram_apply(n, *keep(total(msend, mrecv, n), *spot(n))), 0.0625)
            return 0

        lax.fori_loop(0, SIZE // 5, step, 0)
        group_copy(i_pair, g).start()

    def step_terms(n, c, f):
        power = noise[c]
        br, bi = keep(total(msend, mrecv, n), c, f)
        ir, ii = keep(total(isend, irecv, n), c, f)
        ir, ii = ir + power * br, ii + power * bi
        norm0 = row_sum(br * br + bi * bi)
        alpha = norm0 / row_sum(br * ir + bi * ii)
        first[n, 0], first[n, 1] = alpha * br, alpha * bi
        rr, ri = br - alpha * ir, bi - alpha * ii
        norm = row_sum(rr * rr + ri * ri)
        beta = norm / norm0
        dr, di = rr + beta * br, ri + beta * bi
        second[n, 0], second[n, 1] = dr, di
        return norm, power * row_sum(dr * dr + di * di), dr, di

    def collect(target, pairs):
        value = target[...]
        for n, item in pairs:
            value = jnp.where(lane == n, item, value)
        target[...] = value

    def update_phase(g):
        group_copy(i_pair, g).wait()

        def step(i, _):
            spots = [g * SIZE + 5 * i + k for k in range(5)]
            terms = [step_terms(n, *spot(n)) for n in spots]
            squares = []
            for n, (_norm, _dirsq, dr, di) in zip(spots, terms):
                gr, gi = gram_apply(n, dr, di)
                squares.append(row_sum(dr * gr + di * gi) * 0.0625)
            collect(norm1, [(n, t[0]) for n, t in zip(spots, terms)])
            collect(dirsq, [(n, t[1]) for n, t in zip(spots, terms)])
            collect(qsend.at[0], list(zip(spots, squares)))
            return 0

        lax.fori_loop(0, SIZE // 5, step, 0)

    def square_sum(column):
        square = column * column
        square = square[:16] + square[16:]
        return row_sum((square[:, :128] + square[:, 128:256]) + (square[:, 256:384] + square[:, 384:]))

    ends = (s_id == 0, s_id == n_sc - 1)
    gains = [jnp.where(end, 1.0 / 3.0, 0.25).astype(F32) for end in ends]
    halo_gains = [jnp.where(end, 0.0, 0.25).astype(F32) for end in ends]

    def own_edges(cell):
        return [(2 * cell + side, side, GROUPS * SIZE + 2 * cell + side, side * (BAND - 1)) for side in range(2)]

    def edge_matched(c):
        for copy in halo_copies[4 * c : 4 * c + 4] + other_copies[2 * c : 2 * c + 2]:
            copy.wait()
        for e, side, n, f in own_edges(c):
            mine = adjoint(sample_rows(rx[c, f], 0), edge[e])
            theirs = adjoint(sample_rows(rx_other[c, side], 1), halo[c, side])
            put(msend, n, [u * gains[side] + v * halo_gains[side] for u, v in zip(mine, theirs)], 1.0)
        edge_copy(m_pair, c).start()

    def pack(target, column):
        for a in range(2):
            target[a] = column[16 * a : 16 * a + SYM].astype(BF16)

    def unpack(source):
        pad = jnp.zeros((2, ANT), F32)
        return jnp.concatenate([source[0].astype(F32), pad, source[1].astype(F32), pad], axis=0)

    def edge_products(target, c, real, imag, e, side):
        pack(target.at[c, 0, side], forward(real, imag, edge[e]) * gains[side])
        pack(target.at[c, 1, side], forward(real, imag, halo[c, side]) * halo_gains[side])

    def edge_sums(sent, got, c, side):
        mine = unpack(sent.at[c, 0, side]) + unpack(got.at[c, 1, side])
        theirs = unpack(got.at[c, 0, side]) + unpack(sent.at[c, 1, side])
        return mine, theirs

    def edge_columns(c):
        edge_copy(m_pair, c).wait()
        for e, side, n, f in own_edges(c):
            real, imag = [v.astype(BF16) for v in keep(total(msend, mrecv, n), c, f)]
            edge_products(xsend, c, real, imag, e, side)
        x_copy(c).start()

    def edge_image(c):
        x_copy(c).wait()
        for e, side, n, f in own_edges(c):
            mine, theirs = [v.astype(BF16) for v in edge_sums(xsend, xrecv, c, side)]
            mine, theirs = adjoint(mine, edge[e]), adjoint(theirs, halo[c, side])
            put(isend, n, [u * gains[side] + v * halo_gains[side] for u, v in zip(mine, theirs)], 1.0)
        edge_copy(i_pair, c).start()

    def edge_update(c):
        edge_copy(i_pair, c).wait()
        found = own_edges(c)
        terms = [(n, step_terms(n, c, f)) for e, side, n, f in found]
        collect(norm1, [(n, t[0]) for n, t in terms])
        collect(dirsq, [(n, t[1]) for n, t in terms])
        for (e, side, n, f), (_n, t) in zip(found, terms):
            real, imag = t[2].astype(BF16), t[3].astype(BF16)
            pack(ysend.at[c, side], forward(real, imag, halo[c, side]) * halo_gains[side])
            own2[e] = forward(real, imag, edge[e]) * gains[side]
        y_copy(c).start()

    def edge_norm(c):
        y_copy(c).wait()
        collect(
            qsend.at[1],
            [(n, square_sum(own2[e] + unpack(yrecv.at[c, side]))) for e, side, n, f in own_edges(c)],
        )

    def q_copy(k):
        return remote(qsend.at[k], qrecv.at[k], q_ssem.at[k], q_rsem.at[k], partner)

    qsend[...] = jnp.zeros_like(qsend)
    norm1[...] = jnp.ones_like(norm1)
    dirsq[...] = jnp.ones_like(dirsq)

    def finish(n, c, f):
        alpha = row_sum(jnp.where(lane == n, alphas[n // (GROUPS * SIZE)], 0.0))
        for part in range(2):
            value = first[n, part] + alpha * second[n, part]
            for h in range(2):
                det[c, pl.ds((2 * part + h) * 256 + f * 8, 8), :] = value[8 * h : 8 * h + 8]

    def step_sizes(k):
        q_copy(k).wait()
        alphas[k] = norm1[...] / (qsend[k] + qrecv[k] + dirsq[...])

    def finish_phase(batch, _):
        for k in range(5):
            n = 5 * batch + k
            finish(n, *spot(n))
        return 0

    def edge_blocks(c):
        def strip(i, _):
            rows = pl.ds(pl.multiple_of(i * 64, 64), 64)
            for e, side, n, f in own_edges(c):
                for part in range(2):
                    here, inner = raw[c, f, part, rows, :], raw[c, 1 + side * (BAND - 3), part, rows, :]
                    edge[e, rows, pl.ds(128 * part, 128)] = inner + (here + here)
            return 0

        lax.fori_loop(0, ANT // 64, strip, 0)

    def raw_wait(g):
        raw_copy(g // PER_CELL, lax.rem(g, PER_CELL)).wait()

    raw_wait(0)
    smooth_stage(0, 0)

    def main_step(g, _):
        gram_stage(2 * g, 0)
        smooth_stage(2 * g + 1, 1)
        raw_wait(g + 1)
        gram_stage(2 * g + 1, 1)
        smooth_stage(2 * g + 2, 0)
        group_copy(m_pair, g).start()

        @pl.when(g >= 1)
        def _():
            image_phase(g - 1)

        @pl.when(g >= 2)
        def _():
            update_phase(g - 2)

        @pl.when(g == 2)
        def _():
            edge_blocks(0)
            edge_matched(0)

        @pl.when(g == 3)
        def _():
            edge_columns(0)

        @pl.when(g == 4)
        def _():
            edge_blocks(1)
            edge_matched(1)
            edge_image(0)

        return 0

    last = GROUPS - 1
    lax.fori_loop(0, last, main_step, 0)
    gram_stage(2 * last, 0)
    smooth_stage(2 * last + 1, 1)
    edge_columns(1)
    gram_stage(2 * last + 1, 1)
    group_copy(m_pair, last).start()
    image_phase(last - 1)
    edge_update(0)
    update_phase(last - 2)
    edge_image(1)
    image_phase(last)
    update_phase(last - 1)
    edge_update(1)
    update_phase(last)
    q_copy(0).start()
    edge_norm(0)
    edge_norm(1)
    q_copy(1).start()
    step_sizes(0)
    lax.fori_loop(0, 2 * GROUPS, finish_phase, 0)
    step_sizes(1)
    for c, side, n, f in edges:
        finish(n, c, f)

    def placed(which, c):
        a, s = which // SYM, which % SYM
        return det[c, pl.ds((2 * a + s // 8) * 256 + s % 8, BAND, stride=8), :].astype(BF16)

    for low in range(0, 2 * SYM, 8):
        high = min(low + 8, 2 * SYM)
        table = jnp.concatenate(
            [jnp.concatenate([placed(w, c) for w in range(low, high)], axis=0) for c in range(2)], axis=1
        )
        sent = lax.dot_general(
            onehot[...], table, (((1,), (1,)), ((), ())), preferred_element_type=F32
        )
        sent = sent.astype(BF16).reshape(32, 16, (high - low) * BAND)
        outgoing[:, :, pl.ds(low * BAND, (high - low) * BAND)] = sent

    def target(i):
        k = lax.rem(i + s_id, n_sc)
        return k, c_id * half + lax.rem(k, half)

    def to_self(k):
        return (k // half == c_id) & (c_id * half + lax.rem(k, half) == s_id)

    def parcel(k, other):
        return remote(
            outgoing.at[k], arrived.at[s_id], d_ssem.at[k], d_rsem.at[s_id], (k // half, panel_to(other), other)
        )

    def local_parcel(k):
        return pltpu.make_async_copy(outgoing.at[k], arrived.at[s_id], d_lsem)

    def send(i, _):
        k, other = target(i)

        @pl.when(to_self(k))
        def _():
            local_parcel(k).start()

        @pl.when(jnp.logical_not(to_self(k)))
        def _():
            parcel(k, other).start()

        return 0

    lax.fori_loop(0, n_sc, send, 0)

    def settle(i, _):
        k, other = target(i)

        @pl.when(to_self(k))
        def _():
            local_parcel(k).wait()

        @pl.when(jnp.logical_not(to_self(k)))
        def _():
            parcel(k, other).wait_send()

        @pl.when(jnp.logical_not(from_self(i)))
        def _():
            remote(
                outgoing.at[0], arrived.at[i], d_ssem.at[0], d_rsem.at[i], (origin, panel_to(i), i)
            ).wait_recv()

        return 0

    lax.fori_loop(0, n_sc, settle, 0)


ROWS = 2 * SYM * 16


def assemble_kernel(arrived, out, mixed, order):
    @pl.when(pl.program_id(0) == 0)
    def _():
        to = lax.broadcasted_iota(jnp.int32, (ROWS, ROWS), 0)
        source = lax.broadcasted_iota(jnp.int32, (ROWS, ROWS), 1)
        which, slot = source // 16, lax.rem(source, 16)
        goes = slot * (2 * SYM) + lax.rem(which, SYM) * 2 + which // SYM
        order[...] = jnp.where(to == goes, 1.0, 0.0).astype(BF16)

    lane = lax.broadcasted_iota(jnp.int32, (16, 128), 1)
    for half in range(2):
        for tile in range(7):
            blocks = [arrived[4 * half + k, :, pl.ds(128 * tile, 128)].astype(F32) for k in range(4)]
            for m in range(4):
                value = blocks[m]
                for k in range(4):
                    if k != m:
                        moved = pltpu.roll(blocks[k], (32 * (k - m)) % 128, 1)
                        inside = (lane >= 32 * k) & (lane < 32 * k + 32)
                        value = jnp.where(inside, moved, value)
                mixed[pl.ds((4 * tile + m) * 16, 16), pl.ds(128 * half, 128)] = value.astype(BF16)
    moved = jnp.dot(order[...], mixed[...], preferred_element_type=F32)
    for slot in range(16):
        rows = moved[slot * 2 * SYM : (slot + 1) * 2 * SYM]
        out[slot] = rows.astype(BF16).reshape(SYM, 2, 256)


def body(channel, received, noise_power, user_count, serving_cell):
    vmem = pltpu.VMEM
    keys = serving_cell.transpose(0, 2, 1)
    received = received.transpose(0, 1, 3, 2, 4)
    dma = pltpu.SemaphoreType.DMA
    arrived = pl.pallas_call(
        detect_kernel,
        name="detect",
        out_shape=jax.ShapeDtypeStruct((32, 16, 2 * SYM * BAND), BF16),
        in_specs=[
            pl.BlockSpec(memory_space=pl.ANY),
            pl.BlockSpec(memory_space=pl.ANY),
            pl.BlockSpec(memory_space=pltpu.SMEM),
            pl.BlockSpec(memory_space=pltpu.SMEM),
            pl.BlockSpec(memory_space=vmem),
        ],
        out_specs=pl.BlockSpec(memory_space=pl.ANY),
        scratch_shapes=[
            vmem((2, BAND, 2, ANT, USERS), BF16),
            vmem((2, 5, ANT, 2 * USERS), BF16),
            vmem((GROUPS * SIZE, 2 * USERS, USERS), BF16),
            vmem((4, ANT, 2 * USERS), BF16),
            vmem((2, BAND, 16, 2, ANT), BF16),
            vmem((2, 2, 16, 2, ANT), BF16),
            vmem((5, ANT // 128, 32, 128), F32),
            vmem((2, 2, ANT, 2 * USERS), BF16),
            vmem((UNITS, 2, SYM, USERS), BF16),
            vmem((UNITS, 2, SYM, USERS), BF16),
            vmem((UNITS, 2, SYM, USERS), BF16),
            vmem((UNITS, 2, SYM, USERS), BF16),
            vmem((2, 2, 2, 2, SYM, ANT), BF16),
            vmem((2, 2, 2, 2, SYM, ANT), BF16),
            vmem((2, 2, 2, SYM, ANT), BF16),
            vmem((2, 2, 2, SYM, ANT), BF16),
            vmem((4, 32, ANT), F32),
            vmem((2, 16, 128), F32),
            vmem((2, 16, 128), F32),
            vmem((2, 16, 128), F32),
            vmem((16, 128), F32),
            vmem((16, 128), F32),
            vmem((UNITS, 2, 16, USERS), F32),
            vmem((UNITS, 2, 16, USERS), F32),
            vmem((2, 1024, USERS), F32),
            vmem((512, 2 * USERS), BF16),
            vmem((32, 16, 2 * SYM * BAND), BF16),
            dma((2, PER_CELL + 1)),
            dma((2,)),
            dma((2, 2, 2)),
            dma((2, 2, 2)),
            dma((2, 2)),
            dma((2, 2)),
            dma((GROUPS + 2,)),
            dma((GROUPS + 2,)),
            dma((GROUPS + 2,)),
            dma((GROUPS + 2,)),
            dma((2, 2)),
            dma((2, 2)),
            dma((2,)),
            dma((2,)),
            dma((32,)),
            dma((32,)),
            dma,
        ],
        compiler_params=pltpu.CompilerParams(
            collective_id=0, has_side_effects=True, vmem_limit_bytes=60 * 1024 * 1024
        ),
    )(channel, received, noise_power, user_count, keys)
    routed = pl.pallas_call(
        assemble_kernel,
        name="assemble",
        grid=(4,),
        out_shape=jax.ShapeDtypeStruct((16, SYM, 2, 32 * BAND), BF16),
        in_specs=[pl.BlockSpec((8, 16, 2 * SYM * BAND), lambda i: (i, 0, 0))],
        out_specs=pl.BlockSpec((16, SYM, 2, 256), lambda i: (0, 0, 0, i)),
        scratch_shapes=[vmem((ROWS, 256), BF16), vmem((ROWS, ROWS), BF16)],
    )(arrived)
    return routed.reshape(2, 8, SYM, 2, 32 * BAND).transpose(0, 1, 3, 2, 4)


def solution(mesh):
    return jax.shard_map(
        body,
        mesh=mesh,
        in_specs=(
            P("cell", "sc", None, "panel", None),
            P("cell", "sc", None, None, "panel"),
            P("cell"),
            P("cell", "sc"),
            P("cell", None, None),
        ),
        out_specs=P("cell", "sc", None, None, None),
        check_vma=False,
    )
```
